32 devices in a mesh: dp: 4 (over y, core), fsdp: 8 (over z, x).
Axes of the slice: x: 2, y: 2, z: 4, core: 2. Of those that a mesh axis runs over, the one named last changes fastest.
Arguments:
- tokens: bfloat16 [2, 32, 1024, 768], P(None, ('dp', 'fsdp')), may hold values from -6 to 6
- task_ids: int32 [2, 32, 4], P(None, ('dp', 'fsdp')), may hold values from 0 to 7
- logit_grads: bfloat16 [2, 32, 4, 100], P(None, ('dp', 'fsdp')), may hold values from -6 to 6
- prompts: bfloat16 [8, 50, 768], replicated, may hold values from -6 to 6
- head_weights: bfloat16 [8, 768, 100], replicated, may hold values from -0.21875 to 0.21875
- qkv_weight: bfloat16 [768, 2304], P('fsdp'), may hold values from -0.3125 to 0.3125
- out_weight: bfloat16 [768, 768], P('fsdp'), may hold values from -0.875 to 0.875
- up_weight: bfloat16 [768, 3072], P('fsdp'), may hold values from -0.21875 to 0.21875
- down_weight: bfloat16 [3072, 768], P('fsdp'), may hold values from -0.109375 to 0.109375
- attn_gain: float32 [768], replicated, may hold values from 0.5 to 1.5
- mlp_gain: float32 [768], replicated, may hold values from 0.5 to 1.5
- final_gain: float32 [768], replicated, may hold values from 0.5 to 1.5
Outputs:
- activations: bfloat16 [2, 32, 1024, 768], P(None, ('dp', 'fsdp'))
- input_grads: float32 [2, 32, 1024, 768], P(None, ('dp', 'fsdp'))
- prompt_grads: float32 [8, 50, 768], replicated
- head_grads: float32 [8, 768, 100], replicated
The draws below stay inside these ranges and needn't reach their ends.
All inputs are finite; a program needn't handle non-finite values.
Results may differ from the reference program's by a relative error of at most 0.011.
The reference program's roundings to bfloat16 on the way count: a program that leaves them out, or rounds other values in their place, can miss the bound.
Values may be sent and summed in bfloat16 or wider, within the bound.
No kernel may reach another device: no remote copies, remote signals or barrier semaphores. Data moves between devices by JAX's collectives and lax.ppermute only.
A program may use at most 192 MiB of HBM per device.

```python
import math
import jax
import jax.numpy as jnp
import numpy as np
from jax import lax

D = 768
HEADS = 12
HDIM = 64
FF = 3072
CLASSES = 100
TASKS = 8
PROMPTS = 50
IMG = 247
IMGS_ROW = 4
ROW = 1024
MB = 2
RT = 32


def set_ends(drawn, key, smallest, largest):
    index_at = [jax.random.randint(jax.random.fold_in(key, axis), (), 0, length) for axis, length in enumerate(drawn.shape)]
    main_axis = drawn.shape.index(max(drawn.shape))
    next_to = index_at[:main_axis] + [(index_at[main_axis] + 1) % drawn.shape[main_axis]] + index_at[main_axis + 1:]
    return drawn.at[tuple(index_at)].set(smallest).at[tuple(next_to)].set(largest)


def level_of(key, extent, pieces, smallest, top_value):
    level = 1.0
    for axis_at, shards_of in pieces:
        heights = jax.random.uniform(jax.random.fold_in(jax.random.fold_in(key, 6), axis_at), (shards_of,), jnp.float32, smallest / len(pieces), top_value / len(pieces))
        level = level * jnp.repeat(jnp.exp(heights), extent[axis_at] // shards_of).reshape((-1,) + (1,) * (len(extent) - 1 - axis_at))
    return level


def cumulative_ranks(amount, slope):
    portions = [(1 << 20) // math.isqrt(rank ** slope) + 1 for rank in range(1, amount + 1)]
    spread = 1 + sum(portions) // (1 << 30)
    return np.cumsum(np.array([max(1, weight // spread) for weight in portions]))


def ranked(key, extent, count, slope):
    table = cumulative_ranks(count, slope)
    pick = jax.random.randint(jax.random.fold_in(key, 1), extent, 0, int(table[count - 1]))
    rank = jnp.searchsorted(jnp.asarray(table, jnp.int32), pick, side="right")
    return jax.random.permutation(jax.random.fold_in(key, 2), count)[rank].astype(jnp.int32)


def noise(key, dims, spread, limit, shards=(), held_as=jnp.bfloat16):
    level = level_of(key, dims, shards, -0.22, 0.18) if shards else 1.0
    values = jax.random.normal(key, dims, jnp.float32) * spread * level
    return jnp.minimum(jnp.maximum(values, -limit), limit).astype(held_as)


def setup_inputs(seed: int = 0) -> dict:
    splits = jax.random.split(jax.random.key(seed), 13)
    tokens = noise(splits[0], (MB, RT, ROW, D), 1.0, 6.0, ((1, 32),))
    task_ids = set_ends(ranked(splits[1], (MB, RT, IMGS_ROW), TASKS, 2), jax.random.fold_in(splits[1], 3), 0, TASKS - 1).astype(jnp.int32)
    logit_grads = noise(splits[2], (MB, RT, IMGS_ROW, CLASSES), 1.0, 6.0, ((1, 32),))
    prompts = noise(splits[3], (TASKS, PROMPTS, D), 1.0, 6.0)
    head_weights = noise(splits[4], (TASKS, D, CLASSES), D ** -0.5, 0.21875)
    qkv_weight = noise(splits[5], (D, 3 * D), (D // 2) ** -0.5, 0.3125, ((0, 8),))
    out_weight = noise(splits[6], (D, D), (D // 16) ** -0.5, 0.875, ((0, 8),))
    up_weight = noise(splits[7], (D, FF), D ** -0.5, 0.21875, ((0, 8),))
    down_weight = noise(splits[8], (FF, D), FF ** -0.5, 0.109375, ((0, 8),))
    attn_gain = jnp.clip(1.0 + 0.1 * jax.random.normal(splits[9], (D,), jnp.float32), 0.5, 1.5)
    mlp_gain = jnp.clip(1.0 + 0.1 * jax.random.normal(splits[10], (D,), jnp.float32), 0.5, 1.5)
    final_gain = jnp.clip(1.0 + 0.1 * jax.random.normal(splits[11], (D,), jnp.float32), 0.5, 1.5)
    return dict(tokens=tokens, task_ids=task_ids, logit_grads=logit_grads, prompts=prompts, head_weights=head_weights, qkv_weight=qkv_weight, out_weight=out_weight, up_weight=up_weight, down_weight=down_weight, attn_gain=attn_gain, mlp_gain=mlp_gain, final_gain=final_gain)


EPSILON = 1e-06
PRECISE = lax.Precision.HIGHEST
MASKED_SCORE = -1e+30

@jax.custom_vjp
def low(v):
    return lax.optimization_barrier(v.astype(jnp.bfloat16)).astype(jnp.float32)

@jax.custom_vjp
def low_back(v):
    return v

def low_keep(v):
    return (low(v), None)

def low_pass(kept, grad):
    return (grad,)

def back_keep(v):
    return (v, None)

def back_low(kept, grad):
    return (low(grad),)
low.defvjp(low_keep, low_pass)
low_back.defvjp(back_keep, back_low)

def layer_norm(rows, gain):
    row_mean = lax.optimization_barrier(jnp.mean(rows, axis=-1, keepdims=True))
    centred = rows - row_mean
    return centred * lax.rsqrt(lax.optimization_barrier(jnp.mean(centred * centred, axis=-1, keepdims=True)) + EPSILON) * gain

def gelu_exact(inputs):
    return jax.nn.gelu(inputs, approximate=False)

def forward_rows(rows_in, prompts, head_weights, weights, one_hot):
    qkv_weight, out_weight, up_weight, down_weight, attn_gain, mlp_gain, final_gain = weights
    group_n = rows_in.shape[0]
    chosen = jnp.dot(one_hot.reshape(group_n * IMGS_ROW, TASKS), prompts.reshape(TASKS, PROMPTS * D), precision=PRECISE)
    chosen = chosen.reshape(group_n, IMGS_ROW, PROMPTS, D)
    images = rows_in[:, :IMGS_ROW * IMG].reshape(group_n, IMGS_ROW, IMG, D)
    images = jnp.concatenate([images[:, :, :1], chosen, images[:, :, 1 + PROMPTS:]], axis=2)
    resid = jnp.concatenate([images.reshape(group_n, IMGS_ROW * IMG, D), rows_in[:, IMGS_ROW * IMG:]], axis=1)
    normed = low(layer_norm(resid, attn_gain))
    packed = low_back(low(jnp.einsum('gpd,de->gpe', normed, qkv_weight, precision=PRECISE)))
    queries = packed[..., :D].reshape(group_n, ROW, HEADS, HDIM)
    key_vecs = packed[..., D:2 * D].reshape(group_n, ROW, HEADS, HDIM)
    value_vecs = packed[..., 2 * D:].reshape(group_n, ROW, HEADS, HDIM)
    segment_of = jnp.minimum(jnp.arange(ROW, dtype=jnp.int32) // IMG, IMGS_ROW)
    same_image = segment_of[:, None] == segment_of[None, :]
    scores = low_back(jnp.einsum('gqhd,gkhd->ghqk', queries, key_vecs, precision=PRECISE) * HDIM ** (-0.5))
    attn_probs = low(jax.nn.softmax(jnp.where(same_image, scores, MASKED_SCORE), axis=-1))
    context = jnp.einsum('ghqk,gkhd->gqhd', attn_probs, value_vecs, precision=PRECISE)
    context = low_back(low(context)).reshape(group_n, ROW, D)
    middle = resid + low_back(jnp.einsum('gpd,de->gpe', context, out_weight, precision=PRECISE))
    normed_two = low(layer_norm(middle, mlp_gain))
    pre_act = low_back(jnp.einsum('gpd,df->gpf', normed_two, up_weight, precision=PRECISE))
    activated = low(gelu_exact(pre_act))
    output = middle + low_back(jnp.einsum('gpf,fd->gpd', activated, down_weight, precision=PRECISE))
    class_rows = output[:, :IMGS_ROW * IMG].reshape(group_n, IMGS_ROW, IMG, D)[:, :, 0]
    final_rows = low(layer_norm(class_rows, final_gain)).reshape(group_n * IMGS_ROW, D)
    every = jnp.dot(final_rows, head_weights.transpose(1, 0, 2).reshape(D, TASKS * CLASSES), precision=PRECISE)
    logits = lax.optimization_barrier(jnp.sum(every.reshape(-1, TASKS, CLASSES) * one_hot.reshape(-1, TASKS, 1), axis=1))
    return (output, logits)

def reference(tokens, task_ids, logit_grads, prompts, head_weights, qkv_weight, out_weight, up_weight, down_weight, attn_gain, mlp_gain, final_gain):
    weights = (qkv_weight.astype(jnp.float32), out_weight.astype(jnp.float32), up_weight.astype(jnp.float32), down_weight.astype(jnp.float32), attn_gain.astype(jnp.float32), mlp_gain.astype(jnp.float32), final_gain.astype(jnp.float32))
    one_hot = (task_ids[..., None] == jnp.arange(TASKS, dtype=jnp.int32)).astype(jnp.float32)
    rows_all = tokens.astype(jnp.float32).reshape(-1, 2, ROW, D)
    hot_all = one_hot.reshape(-1, 2, IMGS_ROW, TASKS)
    cot_all = logit_grads.astype(jnp.float32).reshape(-1, 2 * IMGS_ROW, CLASSES)
    prompts_float = prompts.astype(jnp.float32)
    heads_float = head_weights.astype(jnp.float32)

    def step_rows(running, batch_item):
        rows_in, hot_group, cot_group = batch_item

        def forward(rows_arg, prompt_arg, head_arg):
            return forward_rows(rows_arg, prompt_arg, head_arg, weights, hot_group)
        (output, logits), pull_back = jax.vjp(forward, rows_in, prompts_float, heads_float)
        d_rows, d_prompts, d_heads = pull_back((jnp.zeros_like(output), cot_group))
        return ((running[0] + d_prompts, running[1] + d_heads), (output.astype(jnp.bfloat16), d_rows))
    start_sums = (jnp.zeros(prompts.shape, jnp.float32), jnp.zeros(head_weights.shape, jnp.float32))
    (prompt_grads, head_grads), (activations, input_grads) = lax.scan(step_rows, start_sums, (rows_all, hot_all, cot_all))
    return (activations.reshape(tokens.shape), input_grads.reshape(tokens.shape), prompt_grads, head_grads)
```

```python
import functools

import jax
import jax.numpy as jnp
import numpy as np
from jax import lax
from jax.experimental import pallas as pl
from jax.experimental.pallas import tpu as pltpu
from jax.sharding import PartitionSpec as P

D = 768
HEADS = 12
HDIM = 64
FF = 3072
CLASSES = 100
TASKS = 8
PROMPTS = 50
IMG = 247
IMGS_ROW = 4
ROW = 1024
MB = 2

BLOCK = 256
TAIL = BLOCK - IMG
TAIL_AT = IMGS_ROW * IMG
HEADS_PAD = 16
SLOTS = 64
EPSILON = 1e-06
MASKED_SCORE = -1e30
BF16 = jnp.bfloat16
F32 = jnp.float32


def dot(lhs, rhs):
    return lax.dot_general(lhs, rhs, (((1,), (0,)), ((), ())), preferred_element_type=F32)


def dot_t(lhs, rhs):
    return lax.dot_general(lhs, rhs, (((1,), (1,)), ((), ())), preferred_element_type=F32)


def unit_norm(rows):
    centred = rows - jnp.mean(rows, axis=-1, keepdims=True)
    inv_std = lax.rsqrt(jnp.mean(centred * centred, axis=-1, keepdims=True) + EPSILON)
    return centred * inv_std, inv_std


def norm_back(grad_out, unit_rows, inv_std, gain):
    scaled = grad_out * gain
    inner_mean = jnp.mean(scaled * unit_rows, axis=-1, keepdims=True)
    return inv_std * (scaled - jnp.mean(scaled, axis=-1, keepdims=True) - unit_rows * inner_mean)


def gelu(rows):
    return 0.5 * rows * (1.0 + lax.erf(rows * np.float32(np.sqrt(0.5))))


def gelu_slope(rows):
    upper = 0.5 * (1.0 + lax.erf(rows * np.float32(np.sqrt(0.5))))
    return upper + rows * jnp.exp(-0.5 * rows * rows) * np.float32(1.0 / np.sqrt(2.0 * np.pi))


def params(mib):
    return pltpu.CompilerParams(vmem_limit_bytes=mib << 20)


def cost(gflops, mbytes):
    return pl.CostEstimate(flops=int(gflops * 1e9), bytes_accessed=int(mbytes * 1e6), transcendentals=0)


def far(array):
    return pltpu.with_memory_space_constraint(array, pltpu.HBM)


def whole(array):
    return pl.BlockSpec(array.shape, lambda *grid: (0,) * array.ndim, pipeline_mode=pl.Buffered(1))


def make_copies(pairs, sems, first=0):
    return [pltpu.make_async_copy(src, dst, sems.at[first + k]) for k, (src, dst) in enumerate(pairs)]


def start_copies(pairs, sems):
    copies = make_copies(pairs, sems)
    for copy in copies:
        copy.start()
    return copies


def run_copies(pairs, sems):
    for copy in start_copies(pairs, sems):
        copy.wait()


LANES = 128
LANE_BLOCKS = [slice(at, at + LANES) for at in range(0, D, LANES)]


def by_lanes(buf, rows):
    for block, lanes in enumerate(LANE_BLOCKS):
        buf[block] = rows[:, lanes]


def read_strided(buf, start, count):
    at = pl.ds(start, count, stride=TASKS)
    return jnp.concatenate([buf[block, at] for block in range(len(LANE_BLOCKS))], axis=1)


def write_strided(buf, start, rows):
    at = pl.ds(start, rows.shape[0], stride=TASKS)
    for block, lanes in enumerate(LANE_BLOCKS):
        buf[block, at] = rows[:, lanes]


def assemble_kernel(
    ids_ref, tokens_ref, prompts_ref, gain_ref, resid_ref, normed_ref, row_buf, img_buf, prompt_buf
):
    row_at = pl.program_id(0)
    by_lanes(prompt_buf, prompts_ref[...].astype(F32))
    row_buf[...] = tokens_ref[0].astype(F32)
    for img in range(IMGS_ROW):
        img_buf[0 : IMG + 1] = row_buf[img * IMG : img * IMG + IMG + 1]
        img_buf[IMG:BLOCK] = row_buf[TAIL_AT + img * TAIL : TAIL_AT + (img + 1) * TAIL]
        img_buf[1 : 1 + PROMPTS] = read_strided(prompt_buf, ids_ref[row_at, img], PROMPTS)
        rows = img_buf[...]
        at = slice(img * BLOCK, (img + 1) * BLOCK)
        resid_ref[0, at] = rows.astype(BF16)
        unit_rows, _ = unit_norm(rows)
        normed_ref[0, at] = (unit_rows * gain_ref[...]).astype(BF16)


def assemble(ids, tokens, prompts, gain):
    rows_n = tokens.shape[0]
    row_spec = pl.BlockSpec((1, ROW, D), lambda r: (r, 0, 0))
    return pl.pallas_call(
        assemble_kernel,
        grid=(rows_n,),
        in_specs=[pl.BlockSpec(memory_space=pltpu.SMEM), row_spec, whole(prompts), whole(gain)],
        out_specs=[row_spec, row_spec],
        out_shape=[jax.ShapeDtypeStruct(tokens.shape, BF16)] * 2,
        scratch_shapes=[
            pltpu.VMEM((ROW, D), F32),
            pltpu.VMEM((BLOCK, D), F32),
            pltpu.VMEM((len(LANE_BLOCKS), PROMPTS * TASKS, LANES), F32),
        ],
        compiler_params=params(32),
        cost_estimate=cost(0.1, 10),
        name="assemble",
    )(ids, tokens, prompts, gain)


def softmax_pair(queries, keys, values_ext, bias, first_half):
    halves = []
    for scale_row in first_half:
        scores = dot_t(queries * scale_row, keys) + bias
        weights = jnp.exp(scores - jnp.max(scores, axis=-1, keepdims=True)).astype(BF16)
        summed = dot(weights, values_ext)
        halves.append(summed[:, :128] / summed[:, 128:])
    lanes = lax.broadcasted_iota(jnp.int32, halves[0].shape, 1)
    return jnp.where(lanes < HDIM, halves[0], halves[1])


def attend_kernel(plan, normed_ref, resid_ref, gain_ref, *refs):
    pieces, refs = refs[:-11], refs[-11:]
    kv_ref, query_ref, probs_ref, middle_ref, class_ref, normed_two_ref, front_ref = refs[:7]
    packed_buf, tail_buf, tail_context, sems = refs[7:]
    img = pl.program_id(1)
    lane = lax.broadcasted_iota(jnp.int32, (1, 128), 1)
    scale = HDIM ** (-0.5)
    halves = [
        jnp.where(lane < HDIM, scale, 0.0).astype(BF16),
        jnp.where(lane < HDIM, 0.0, scale).astype(BF16),
    ]

    @pl.when((pl.program_id(0) == 0) & (img == 0))
    def _():
        run_copies(plan(pieces, front_ref), sems)

    @pl.when(img == 0)
    def _():
        ends = [normed_ref[0, (at + 1) * BLOCK - 16 : (at + 1) * BLOCK, :] for at in range(IMGS_ROW)]
        tail_buf[...] = dot(jnp.concatenate(ends, axis=0), front_ref[:, : 3 * D]).astype(BF16)
        tail_at = lax.broadcasted_iota(jnp.int32, (1, 16 * IMGS_ROW), 1)
        tail_bias = jnp.where(tail_at % 16 >= 16 - TAIL, 0.0, MASKED_SCORE)
        tail_ones = jnp.ones((16 * IMGS_ROW, 128), BF16)
        for pair in range(HEADS // 2):
            q, k, v = (tail_buf[:, part * D + pair * 128 : part * D + (pair + 1) * 128] for part in range(3))
            tail_context[:, pair * 128 : (pair + 1) * 128] = softmax_pair(
                q, k, jnp.concatenate([v, tail_ones], axis=1), tail_bias, halves
            )

    tokens = normed_ref[0, pl.ds(pl.multiple_of(img * BLOCK, BLOCK), BLOCK), :]
    for part in range(3):
        cols = slice(part * D, (part + 1) * D)
        packed_buf[:, cols] = dot(tokens, front_ref[:, cols]).astype(BF16)
    kv_ref[0] = packed_buf[:, D:]
    query_ref[0] = packed_buf[:16, :D]
    key_at = lax.broadcasted_iota(jnp.int32, (1, BLOCK), 1)
    bias = jnp.where(key_at < IMG, 0.0, MASKED_SCORE)
    queries = packed_buf[0:1, :D] * head_rows_mask().astype(BF16) * np.float32(scale).astype(BF16)
    scores = dot_t(queries, packed_buf[:, D : 2 * D]) + bias
    probs = jnp.exp(scores - jnp.max(scores, axis=-1, keepdims=True))
    probs_ref[0] = probs / jnp.sum(probs, axis=-1, keepdims=True)
    ones = jnp.ones((BLOCK, 128), BF16)
    is_tail = lax.broadcasted_iota(jnp.int32, (16, D), 0) >= 16 - TAIL
    context = []
    for pair in range(HEADS // 2):
        q, k, v = (packed_buf[:, part * D + pair * 128 : part * D + (pair + 1) * 128] for part in range(3))
        context.append(softmax_pair(q, k, jnp.concatenate([v, ones], axis=1), bias, halves))
    context = jnp.concatenate(context, axis=1)
    tail = tail_context[pl.ds(pl.multiple_of(img * 16, 16), 16), :]
    last = jnp.where(is_tail, tail, context[BLOCK - 16 :])
    context = jnp.concatenate([context[: BLOCK - 16], last], axis=0).astype(BF16)
    middle = resid_ref[0].astype(F32) + dot(context, front_ref[:, 3 * D :])
    middle_ref[...] = middle
    class_ref[0] = middle[:8]
    normed_two_ref[...] = (unit_norm(middle)[0] * gain_ref[...]).astype(BF16)


def head_rows_mask():
    return (
        lax.broadcasted_iota(jnp.int32, (HEADS_PAD, D), 1) // HDIM
        == lax.broadcasted_iota(jnp.int32, (HEADS_PAD, D), 0)
    ).astype(F32)


def attend(normed, resid, gain, pieces, plan, copies_n):
    rows_n = normed.shape[0]
    images = rows_n * IMGS_ROW
    flat = lambda r, i: (r * IMGS_ROW + i, 0)
    cube = lambda r, i: (r * IMGS_ROW + i, 0, 0)
    front = jax.ShapeDtypeStruct((D, 4 * D), BF16)
    outs = [
        (images, BLOCK, 2 * D, BF16),
        (images, 16, D, BF16),
        (images, HEADS_PAD, BLOCK, F32),
        (images * BLOCK, D, F32),
        (images, 8, D, F32),
        (images * BLOCK, D, BF16),
    ]
    specs = [
        pl.BlockSpec((1, *o[1:-1]), cube) if len(o) == 4 else pl.BlockSpec((BLOCK, D), flat) for o in outs
    ]
    return pl.pallas_call(
        functools.partial(attend_kernel, plan),
        grid=(rows_n, IMGS_ROW),
        in_specs=[
            pl.BlockSpec((1, ROW, D), lambda r, i: (r, 0, 0)),
            pl.BlockSpec((1, BLOCK, D), lambda r, i: (r, i, 0)),
            whole(gain),
        ]
        + [pl.BlockSpec(memory_space=pltpu.HBM)] * len(pieces),
        out_specs=[*specs, whole(front)],
        out_shape=[*(jax.ShapeDtypeStruct(o[:-1], o[-1]) for o in outs), front],
        scratch_shapes=[
            pltpu.VMEM((BLOCK, 3 * D), BF16),
            pltpu.VMEM((16 * IMGS_ROW, 3 * D), BF16),
            pltpu.VMEM((16 * IMGS_ROW, D), F32),
            pltpu.SemaphoreType.DMA((copies_n,)),
        ],
        compiler_params=params(40),
        cost_estimate=cost(16, 30),
        name="attend",
    )(far(normed), far(resid), gain, *pieces)


def class_kernel(
    plans, ids_ref, middle_ref, queries_ref, probs_ref, grads_ref, heads_ref,
    attn_gain_ref, mlp_gain_ref, final_gain_ref, kv_hbm, front_hbm, *refs,
):
    feed_refs = refs[:-16]
    (
        sent_ref, weights_ref, routes_ref, d_class_ref, d_middle_ref, up_ref, down_ref,
        q_buf, c_buf, dq_buf, score_slots, prob_slots, front_ref, kv_ref, sems, feed_sems,
    ) = refs[-16:]
    images = middle_ref.shape[0]
    up_plan, down_plan = plans
    up_pairs, down_pairs = sum(up_plan(feed_refs, up_ref), []), sum(down_plan(feed_refs, down_ref), [])
    feed_copies = start_copies(up_pairs + down_pairs, feed_sems)
    front_copy = pltpu.make_async_copy(front_hbm, front_ref, sems.at[0])
    front_copy.start()
    kv_copy = pltpu.make_async_copy(kv_hbm, kv_ref, sems.at[1])
    kv_copy.start()
    spread = (
        lax.broadcasted_iota(jnp.int32, (128, CLASSES * TASKS), 1) // TASKS
        == lax.broadcasted_iota(jnp.int32, (128, CLASSES * TASKS), 0)
    ).astype(F32).astype(BF16)
    task_at = lax.broadcasted_iota(jnp.int32, (images, CLASSES * TASKS), 1) % TASKS
    chosen = jnp.where(ids_ref[...] == task_at, dot(grads_ref[...], spread), 0.0).astype(BF16)
    d_final = dot(chosen, heads_ref[...])
    mlp_gain, final_gain = mlp_gain_ref[...], final_gain_ref[...]
    middle = middle_ref[:, 0, :]
    unit_mlp, inv_mlp = unit_norm(middle)
    for copy in feed_copies[: len(up_pairs)]:
        copy.wait()
    pre = dot((unit_mlp * mlp_gain).astype(BF16), up_ref[...])
    activated = gelu(pre).astype(BF16)
    for copy in feed_copies[len(up_pairs) :]:
        copy.wait()
    output = middle + dot(activated, down_ref[...])
    unit_fin, inv_fin = unit_norm(output)
    sent_ref[:, 2 * D : 3 * D] = (unit_fin * final_gain).astype(BF16)
    d_output = norm_back(d_final, unit_fin, inv_fin, final_gain)
    d_act = dot_t(d_output.astype(BF16), down_ref[...])
    d_pre = (d_act * gelu_slope(pre)).astype(BF16)
    d_middle = d_output + norm_back(dot_t(d_pre, up_ref[...]), unit_mlp, inv_mlp, mlp_gain)
    d_middle_ref[...] = d_middle
    front_copy.wait()
    d_context = dot_t(d_middle.astype(BF16), front_ref[:, 3 * D :]).astype(BF16)
    sent_ref[:, 3 * D : 4 * D] = d_context
    of_head = head_rows_mask()
    own = of_head.astype(BF16)
    scale = HDIM ** (-0.5)
    kv_copy.wait()
    for img in range(images):
        at = slice(img * HEADS_PAD, (img + 1) * HEADS_PAD)
        query = queries_ref[img, 0:1, :]
        sent_ref[img : img + 1, :D] = query
        q_buf[at] = query * own * np.float32(scale).astype(BF16)
        d_rows = d_context[img : img + 1] * own
        c_buf[at] = d_rows
        keys, values = kv_ref[img, :, :D], kv_ref[img, :, D:]
        probs = probs_ref[img]
        d_probs = dot_t(d_rows, values)
        d_scores = probs * (d_probs - jnp.sum(probs * d_probs, axis=-1, keepdims=True))
        score_slots[at] = d_scores[:, :128]
        prob_slots[at] = probs[:, :128]
        d_scores = d_scores.astype(BF16)
        weights_ref[img, :HEADS_PAD] = d_scores
        weights_ref[img, HEADS_PAD:] = probs.astype(BF16)
        dq_buf[img : img + 1] = jnp.sum(dot(d_scores, keys) * of_head, axis=0, keepdims=True) * scale
    lane = lax.broadcasted_iota(jnp.int32, (images, 128), 1)
    for slots, start in ((prob_slots, D), (score_slots, 4 * D)):
        for pair in range(HEADS // 2):
            first, second = (slots[pl.ds(2 * pair + h, images, stride=HEADS_PAD)] for h in range(2))
            both = jnp.where(lane < SLOTS, first, pltpu.roll(second, SLOTS, 1))
            sent_ref[:, start + pair * 128 : start + (pair + 1) * 128] = both.astype(BF16)
    sent_ref[:, 5 * D :] = grads_ref[...]
    by_key = dot_t(q_buf[...], front_ref[:, D : 2 * D]).astype(BF16)
    by_value = dot_t(c_buf[...], front_ref[:, 2 * D : 3 * D]).astype(BF16)
    for img in range(images):
        at = slice(img * HEADS_PAD, (img + 1) * HEADS_PAD)
        routes_ref[img, :HEADS_PAD] = by_key[at]
        routes_ref[img, HEADS_PAD:] = by_value[at]
    d_class_ref[...] = dot_t(dq_buf[...].astype(BF16), front_ref[:, :D])


SENT = 5 * D + 128


def class_path(ids, middle, queries, probs, grads, heads, gains, kv, front, feed_weights):
    images = middle.shape[0]
    operands = (ids, middle, queries, probs, grads, heads, *gains)
    feed_arrays, plans, copies_n = feed_weights
    remote = (kv, front, *feed_arrays)
    outs = [
        jax.ShapeDtypeStruct((images, SENT), BF16),
        jax.ShapeDtypeStruct((images, 2 * HEADS_PAD, BLOCK), BF16),
        jax.ShapeDtypeStruct((images, 2 * HEADS_PAD, D), BF16),
        jax.ShapeDtypeStruct((images, D), F32),
        jax.ShapeDtypeStruct((images, D), F32),
    ]
    near = [pltpu.VMEM((D, FF), BF16), pltpu.VMEM((FF, D), BF16)]
    return pl.pallas_call(
        functools.partial(class_kernel, plans),
        in_specs=[pl.BlockSpec(memory_space=pltpu.VMEM)] * len(operands)
        + [pl.BlockSpec(memory_space=pltpu.HBM)] * len(remote),
        out_specs=[pl.BlockSpec(memory_space=pltpu.VMEM)] * (len(outs) + 2),
        out_shape=outs + near,
        scratch_shapes=[
            pltpu.VMEM((images * HEADS_PAD, D), BF16),
            pltpu.VMEM((images * HEADS_PAD, D), BF16),
            pltpu.VMEM((images, D), F32),
            pltpu.VMEM((images * HEADS_PAD, 128), F32),
            pltpu.VMEM((images * HEADS_PAD, 128), F32),
            pltpu.VMEM((D, 4 * D), BF16),
            pltpu.VMEM((images, BLOCK, 2 * D), BF16),
            pltpu.SemaphoreType.DMA((2,)),
            pltpu.SemaphoreType.DMA((copies_n,)),
        ],
        compiler_params=params(40),
        cost_estimate=cost(8, 30),
        name="class_path",
    )(*operands, *remote)


FF_STEP = 768


def feed_kernel(normed_ref, middle_ref, up_ref, down_ref, *refs):
    out_ref, row_buf = refs[-2:]
    img = pl.program_id(1)
    rows = normed_ref[...]
    total = middle_ref[...]
    for step in range(FF // FF_STEP):
        at = slice(step * FF_STEP, (step + 1) * FF_STEP)
        total = total + dot(gelu(dot(rows, up_ref[:, at])).astype(BF16), down_ref[at, :])
    for at in range(IMGS_ROW):

        @pl.when(img == at)
        def _():
            row_buf[at * IMG : (at + 1) * IMG] = total[:IMG]
            row_buf[TAIL_AT + at * TAIL : TAIL_AT + (at + 1) * TAIL] = total[IMG:]

    @pl.when(img == IMGS_ROW - 1)
    def _():
        out_ref[0] = row_buf[...].astype(BF16)


def feed(normed, middle, up_all, down_all, first, count, chain):
    rows_n = normed.shape[0] // ROW
    spec = pl.BlockSpec((BLOCK, D), lambda r, i: ((r + first) * IMGS_ROW + i, 0))
    chained = [] if chain is None else [chain]
    return pl.pallas_call(
        feed_kernel,
        grid=(count, IMGS_ROW),
        in_specs=[spec, spec]
        + [pl.BlockSpec(memory_space=pltpu.VMEM)] * 2
        + [pl.BlockSpec(memory_space=pltpu.HBM)] * len(chained),
        out_specs=pl.BlockSpec((1, ROW, D), lambda r, i: (r + first, 0, 0)),
        out_shape=jax.ShapeDtypeStruct((rows_n, ROW, D), BF16),
        input_output_aliases={} if chain is None else {4: 0},
        scratch_shapes=[pltpu.VMEM((ROW, D), F32)],
        compiler_params=params(24),
        cost_estimate=cost(10 * count, 20),
        name="feed",
    )(far(normed), far(middle), up_all, down_all, *chained)


def token_grads_kernel(resid_ref, weights_ref, routes_ref, d_class_ref, d_middle_ref, gain_ref, out_ref):
    row_at = pl.program_id(0)
    gain = gain_ref[...]
    place = lax.broadcasted_iota(jnp.int32, (BLOCK, 1), 0)
    is_class = (place == 0).astype(F32)
    keep = jnp.where((place == 0) | (place > PROMPTS), 1.0, 0.0)
    for img in range(IMGS_ROW):
        one = pl.ds(row_at * IMGS_ROW + img, 1)
        unit_rows, inv_std = unit_norm(resid_ref[0, img * BLOCK : (img + 1) * BLOCK].astype(F32))
        d_normed = lax.dot_general(
            weights_ref[img], routes_ref[img], (((0,), (0,)), ((), ())), preferred_element_type=F32
        )
        d_normed = d_normed + is_class * d_class_ref[one]
        d_resid = norm_back(d_normed, unit_rows, inv_std, gain) + is_class * d_middle_ref[one]
        out_ref[0, img * IMG : (img + 1) * IMG] = (d_resid * keep)[:IMG]
    out_ref[0, TAIL_AT:] = jnp.zeros((ROW - TAIL_AT, D), F32)


def token_grads(resid, weights, routes, d_class, d_middle, gain):
    rows_n = resid.shape[0]
    row_spec = pl.BlockSpec((1, ROW, D), lambda r: (r, 0, 0))
    img_spec = lambda width: pl.BlockSpec((IMGS_ROW, 2 * HEADS_PAD, width), lambda r: (r, 0, 0))
    return pl.pallas_call(
        token_grads_kernel,
        grid=(rows_n,),
        in_specs=[row_spec, img_spec(BLOCK), img_spec(D), whole(d_class), whole(d_middle), whole(gain)],
        out_specs=row_spec,
        out_shape=jax.ShapeDtypeStruct(resid.shape, F32),
        compiler_params=params(32),
        cost_estimate=cost(0.5, 20),
        name="token_grads",
    )(far(resid), weights, routes, d_class, d_middle, gain)


def sums_kernel(front_ref, prompts_ref, gain_ref, *refs):
    parts, (prompt_out, head_out, all_buf, sum_buf, head_buf, prompt_buf, sems) = refs[:-7], refs[-7:]
    rows = parts[0].shape[0]
    run_copies([(part, all_buf.at[pl.ds(at * rows, rows), :]) for at, part in enumerate(parts)], sems)
    scale = np.float32(HDIM ** (-0.5)).astype(BF16)
    column = lambda at: all_buf[:, at * D : (at + 1) * D]
    by_class = all_buf[:, 5 * D :].T
    ids = by_class[CLASSES : CLASSES + 1].astype(F32)
    masks = [(ids == task).astype(F32).astype(BF16) for task in range(TASKS)]
    finals = column(2)
    for task in range(TASKS):
        write_strided(head_buf, task, dot(by_class * masks[task], finals)[:CLASSES])
    for block, lanes in enumerate(LANE_BLOCKS):
        head_out[:, lanes] = head_buf[block]
    lane = lax.broadcasted_iota(jnp.int32, (SLOTS, 128), 1)
    for side, (slots, lane_rows) in enumerate(((column(4), column(0) * scale), (column(1), column(3)))):
        slots = slots.T
        for pair in range(HEADS // 2):
            at = slice(pair * 128, (pair + 1) * 128)
            summed = dot(jnp.concatenate([slots[at] * mask for mask in masks], axis=0), lane_rows[:, at])
            for task in range(TASKS):
                first, second = (summed[task * 128 + h * SLOTS : task * 128 + (h + 1) * SLOTS] for h in range(2))
                sum_buf[task * SLOTS : (task + 1) * SLOTS, side * D + pair * 128 : side * D + (pair + 1) * 128] = (
                    jnp.where(lane < HDIM, first, second).astype(BF16)
                )
    d_normed = dot_t(sum_buf[...], front_ref[:, D : 3 * D])
    by_lanes(prompt_buf, prompts_ref[...].astype(F32))
    for task in range(TASKS):
        unit_rows, inv_std = unit_norm(read_strided(prompt_buf, task, PROMPTS))
        d_task = d_normed[task * SLOTS + 1 : task * SLOTS + 1 + PROMPTS]
        write_strided(prompt_buf, task, norm_back(d_task, unit_rows, inv_std, gain_ref[...]))
    for block, lanes in enumerate(LANE_BLOCKS):
        prompt_out[:, lanes] = prompt_buf[block]


def sums(front, prompts, gain, parts):
    operands = (front, prompts, gain)
    outs = [
        jax.ShapeDtypeStruct((PROMPTS * TASKS, D), F32),
        jax.ShapeDtypeStruct((CLASSES * TASKS, D), F32),
    ]
    images = sum(part.shape[0] for part in parts)
    return pl.pallas_call(
        sums_kernel,
        grid=(1,),
        in_specs=[whole(o) for o in operands] + [pl.BlockSpec(memory_space=pltpu.HBM)] * len(parts),
        out_specs=[whole(o) for o in outs],
        out_shape=outs,
        scratch_shapes=[
            pltpu.VMEM((images, SENT), BF16),
            pltpu.VMEM((TASKS * SLOTS, 2 * D), BF16),
            pltpu.VMEM((len(LANE_BLOCKS), CLASSES * TASKS, LANES), F32),
            pltpu.VMEM((len(LANE_BLOCKS), PROMPTS * TASKS, LANES), F32),
            pltpu.SemaphoreType.DMA((len(parts),)),
        ],
        compiler_params=params(56),
        cost_estimate=cost(5, 15),
        name="sums",
    )(*operands, *parts)


def gather_rows(shard, dp):
    part = shard.shape[0] // dp
    mine = lax.dynamic_slice_in_dim(shard, lax.axis_index("dp") * part, part, 0)
    return lax.all_gather(mine, ("fsdp", "dp"), axis=0, tiled=True)


def copy_whole(at):
    return lambda refs, dst: [(refs[at], dst)]


def places():
    d, f = lax.axis_index("dp"), lax.axis_index("fsdp")
    return d // 2, d % 2, f // 2, f % 2


def exchange(value, dy=0, dc=0, dz=0, dx=0):
    pairs = []
    for at in range(32):
        y, c, z, x = at // 16, at // 8 % 2, at // 2 % 4, at % 2
        pairs.append((at, (((y ^ dy) * 2 + (c ^ dc)) * 4 + (z ^ dz)) * 2 + (x ^ dx)))
    return lax.ppermute(value, ("dp", "fsdp"), pairs)


HALF_COLS = 2 * D


def fetch_front(shard, beside):
    y, c, _, _ = places()
    mine = lax.dynamic_slice(shard, (y * 48, c * HALF_COLS), (48, HALF_COLS))
    along_z = [exchange(mine, dz=r) for r in (1, 2, 3)]
    half = lax.dynamic_slice(shard, (0, c * HALF_COLS), (96, HALF_COLS))
    own_x = exchange(half, dx=1)
    column, *beside = lax.optimization_barrier((jnp.concatenate(along_z, axis=0), *beside))
    over_x, over_y = exchange(column, dx=1), exchange(column, dy=1)
    diag_y, diag_x = exchange(over_x[:80], dy=1), exchange(over_y[80:], dx=1)
    near = [own_x, column, over_x, over_y, diag_y, diag_x]
    pieces = [shard] + near + [exchange(piece, dc=1) for piece in near]

    def plan(refs, dst):
        y, c, z, x = places()
        pairs = [(refs[0], dst.at[pl.ds(pl.multiple_of((z * 2 + x) * 96, 96), 96), :])]
        for side in range(2):
            cols = pl.ds(pl.multiple_of((c ^ side) * HALF_COLS, 128), HALF_COLS)
            own_x, column, over_x, over_y, diag_y, diag_x = refs[1 + 6 * side : 7 + 6 * side]

            def add(ref, start, count, r, x_at, y_at, within=0):
                row = ((z ^ r) * 2 + x_at) * 96 + y_at * 48 + within
                pairs.append((ref.at[pl.ds(start, count), :], dst.at[pl.ds(pl.multiple_of(row, 16), count), cols]))

            add(own_x, 0, 96, 0, x ^ 1, 0)
            for r in (1, 2, 3):
                start = (r - 1) * 48
                add(column, start, 48, r, x, y)
                add(over_x, start, 48, r, x ^ 1, y)
                add(over_y, start, 48, r, x, y ^ 1)
            add(diag_y, 0, 48, 1, x ^ 1, y ^ 1)
            add(diag_y, 48, 32, 2, x ^ 1, y ^ 1)
            add(diag_x, 0, 16, 2, x ^ 1, y ^ 1, 32)
            add(diag_x, 16, 48, 3, x ^ 1, y ^ 1)
        return pairs

    return (pieces, plan, 29), beside


def fetch_rest(up_shard, down_shard):
    d = lax.axis_index("dp")
    up_part = lax.dynamic_slice(up_shard, (0, d * D), (96, D))
    down_part = lax.dynamic_slice_in_dim(down_shard, d * 96, 96, 0)
    gathered = lax.all_gather(jnp.concatenate([up_part, down_part], axis=0), ("fsdp", "dp"), axis=0)

    def up_plan(refs, dst):
        return [
            [(refs[0].at[4 * f + d, 0:96, :], dst.at[96 * f : 96 * f + 96, D * d : D * d + D]) for f in range(8)]
            for d in range(4)
        ]

    def down_plan(refs, dst):
        return [
            [(refs[0].at[at, 96:192, :], dst.at[96 * at : 96 * at + 96]) for at in range(8 * d, 8 * d + 8)]
            for d in range(4)
        ]

    return [gathered], (up_plan, down_plan), 64


def share_rows(rows, works):
    done, parts = None, [rows]
    for work, shifts in zip(works, ([dict(dz=r) for r in (1, 2, 3)], [dict(dx=1)], [dict(dy=1)])):
        rows = jnp.concatenate(parts, axis=0) if len(parts) > 1 else rows
        if done is not None:
            rows, done = lax.optimization_barrier((rows, done))
        parts = [rows] + [exchange(rows, **shift) for shift in shifts]
        done = work(done)
    *parts, done = lax.optimization_barrier((*parts, done))
    return parts + [exchange(part, dc=1) for part in parts], done


def body(
    tuned, dp, tokens, task_ids, logit_grads, prompts, head_weights, qkv_weight, out_weight, up_weight, down_weight,
    attn_gain, mlp_gain, final_gain,
):
    rows_n = tokens.shape[0] * tokens.shape[1]
    images = rows_n * IMGS_ROW
    front_shard = jnp.concatenate([qkv_weight, out_weight], axis=1)
    gains = [gain.reshape(1, D) for gain in (attn_gain, mlp_gain, final_gain)]
    ids = task_ids.reshape(rows_n, IMGS_ROW)
    prompt_rows = prompts.transpose(1, 0, 2).reshape(PROMPTS * TASKS, D)
    resid, normed = assemble(ids, tokens.reshape(rows_n, ROW, D), prompt_rows, gains[0])
    if tuned:
        front_pieces, (resid, normed) = fetch_front(front_shard, (resid, normed))
        feed_weights = fetch_rest(up_weight, down_weight)
    else:
        front_pieces = [gather_rows(front_shard, dp)], copy_whole(0), 1
        plans = tuple(lambda refs, dst, at=at: [copy_whole(at)(refs, dst)] for at in range(2))
        feed_weights = [gather_rows(w, dp) for w in (up_weight, down_weight)], plans, 2
    ids_col = ids.reshape(images, 1)
    head_rows = head_weights.transpose(2, 0, 1).reshape(CLASSES * TASKS, D)
    grads = jnp.concatenate(
        [logit_grads.reshape(images, CLASSES), jnp.broadcast_to(ids_col, (images, 128 - CLASSES)).astype(BF16)], axis=1
    )
    kv, queries, probs, middle, class_middle, normed_two, front = attend(normed, resid, gains[1], *front_pieces)
    sent, weights, routes, d_class, d_middle, up_all, down_all = class_path(
        ids_col, class_middle, queries, probs, grads, head_rows, gains, kv, front, feed_weights
    )
    first_n = rows_n // 2

    def grads_work(done):
        return token_grads(resid, weights, routes, d_class, d_middle, gains[0]), None

    def feed_work(start, count):
        return lambda done: (done[0], feed(normed_two, middle, up_all, down_all, start, count, done[1]))

    works = grads_work, feed_work(0, first_n), feed_work(first_n, rows_n - first_n)
    if tuned:
        parts, (input_grads, activations) = share_rows(sent, works)
    else:
        parts = [lax.all_gather(sent, ("dp", "fsdp"), axis=0, tiled=True)]
        input_grads, activations = works[2](works[1](works[0](None)))
    prompt_out, head_out = sums(front, prompt_rows, gains[0], parts)
    return (
        activations.reshape(tokens.shape),
        input_grads.reshape(tokens.shape),
        prompt_out.reshape(PROMPTS, TASKS, D).transpose(1, 0, 2),
        head_out.reshape(CLASSES, TASKS, D).transpose(1, 2, 0),
    )


def solution(mesh):
    rows = P(None, ("dp", "fsdp"), None, None)
    in_specs = (rows, P(None, ("dp", "fsdp"), None), rows, P(), P(), *(P("fsdp", None),) * 4, P(), P(), P())
    return jax.shard_map(
        functools.partial(body, dict(mesh.shape) == {"dp": 4, "fsdp": 8}, mesh.shape["dp"]),
        mesh=mesh,
        in_specs=in_specs,
        out_specs=(rows, rows, P(), P()),
        check_vma=False,
    )
```

```python
import functools

import jax
import jax.numpy as jnp
import numpy as np
from jax import lax
from jax.experimental import pallas as pl
from jax.experimental.pallas import tpu as pltpu
from jax.sharding import PartitionSpec as P

D = 768
HEADS = 12
HDIM = 64
FF = 3072
CLASSES = 100
TASKS = 8
PROMPTS = 50
IMG = 247
IMGS_ROW = 4
ROW = 1024
MB = 2

BLOCK = 256
TAIL = BLOCK - IMG
TAIL_AT = IMGS_ROW * IMG
HEADS_PAD = 16
SLOTS = 64
EPSILON = 1e-06
MASKED_SCORE = -1e30
BF16 = jnp.bfloat16
F32 = jnp.float32


def dot(lhs, rhs):
    return lax.dot_general(lhs, rhs, (((1,), (0,)), ((), ())), preferred_element_type=F32)


def dot_t(lhs, rhs):
    return lax.dot_general(lhs, rhs, (((1,), (1,)), ((), ())), preferred_element_type=F32)


def unit_norm(rows):
    centred = rows - jnp.mean(rows, axis=-1, keepdims=True)
    inv_std = lax.rsqrt(jnp.mean(centred * centred, axis=-1, keepdims=True) + EPSILON)
    return centred * inv_std, inv_std


def norm_back(grad_out, unit_rows, inv_std, gain):
    scaled = grad_out * gain
    inner_mean = jnp.mean(scaled * unit_rows, axis=-1, keepdims=True)
    return inv_std * (scaled - jnp.mean(scaled, axis=-1, keepdims=True) - unit_rows * inner_mean)


def gelu(rows):
    return 0.5 * rows * (1.0 + lax.erf(rows * np.float32(np.sqrt(0.5))))


def gelu_slope(rows):
    upper = 0.5 * (1.0 + lax.erf(rows * np.float32(np.sqrt(0.5))))
    return upper + rows * jnp.exp(-0.5 * rows * rows) * np.float32(1.0 / np.sqrt(2.0 * np.pi))


def params(mib):
    return pltpu.CompilerParams(vmem_limit_bytes=mib << 20)


def cost(gflops, mbytes):
    return pl.CostEstimate(flops=int(gflops * 1e9), bytes_accessed=int(mbytes * 1e6), transcendentals=0)


def far(array):
    return pltpu.with_memory_space_constraint(array, pltpu.HBM)


def whole(array):
    return pl.BlockSpec(array.shape, lambda *grid: (0,) * array.ndim, pipeline_mode=pl.Buffered(1))


def make_copies(pairs, sems, first=0):
    return [pltpu.make_async_copy(src, dst, sems.at[first + k]) for k, (src, dst) in enumerate(pairs)]


def start_copies(pairs, sems):
    copies = make_copies(pairs, sems)
    for copy in copies:
        copy.start()
    return copies


def run_copies(pairs, sems):
    for copy in start_copies(pairs, sems):
        copy.wait()


LANES = 128
LANE_BLOCKS = [slice(at, at + LANES) for at in range(0, D, LANES)]


def by_lanes(buf, rows):
    for block, lanes in enumerate(LANE_BLOCKS):
        buf[block] = rows[:, lanes]


def read_strided(buf, start, count):
    at = pl.ds(start, count, stride=TASKS)
    return jnp.concatenate([buf[block, at] for block in range(len(LANE_BLOCKS))], axis=1)


def write_strided(buf, start, rows):
    at = pl.ds(start, rows.shape[0], stride=TASKS)
    for block, lanes in enumerate(LANE_BLOCKS):
        buf[block, at] = rows[:, lanes]


def assemble_kernel(
    ids_ref, tokens_ref, prompts_ref, gain_ref, resid_ref, normed_ref, row_buf, img_buf, prompt_buf
):
    row_at = pl.program_id(0)
    by_lanes(prompt_buf, prompts_ref[...].astype(F32))
    row_buf[...] = tokens_ref[0].astype(F32)
    for img in range(IMGS_ROW):
        img_buf[0 : IMG + 1] = row_buf[img * IMG : img * IMG + IMG + 1]
        img_buf[IMG:BLOCK] = row_buf[TAIL_AT + img * TAIL : TAIL_AT + (img + 1) * TAIL]
        img_buf[1 : 1 + PROMPTS] = read_strided(prompt_buf, ids_ref[row_at, img], PROMPTS)
        rows = img_buf[...]
        at = slice(img * BLOCK, (img + 1) * BLOCK)
        resid_ref[0, at] = rows.astype(BF16)
        unit_rows, _ = unit_norm(rows)
        normed_ref[0, at] = (unit_rows * gain_ref[...]).astype(BF16)


def assemble(ids, tokens, prompts, gain):
    rows_n = tokens.shape[0]
    row_spec = pl.BlockSpec((1, ROW, D), lambda r: (r, 0, 0))
    return pl.pallas_call(
        assemble_kernel,
        grid=(rows_n,),
        in_specs=[pl.BlockSpec(memory_space=pltpu.SMEM), row_spec, whole(prompts), whole(gain)],
        out_specs=[row_spec, row_spec],
        out_shape=[pltpu.HBM(tokens.shape, BF16)] * 2,
        scratch_shapes=[
            pltpu.VMEM((ROW, D), F32),
            pltpu.VMEM((BLOCK, D), F32),
            pltpu.VMEM((len(LANE_BLOCKS), PROMPTS * TASKS, LANES), F32),
        ],
        compiler_params=params(20),
        cost_estimate=cost(0.1, 10),
        name="assemble",
    )(ids, tokens, prompts, gain)


def softmax_pair(queries, keys, values_ext, bias, first_half):
    halves = []
    for scale_row in first_half:
        scores = dot_t(queries * scale_row, keys) + bias
        weights = jnp.exp(scores - jnp.max(scores, axis=-1, keepdims=True)).astype(BF16)
        summed = dot(weights, values_ext)
        halves.append(summed[:, :128] / summed[:, 128:])
    lanes = lax.broadcasted_iota(jnp.int32, halves[0].shape, 1)
    return jnp.where(lanes < HDIM, halves[0], halves[1])


def attend_kernel(plan, normed_ref, resid_ref, gain_ref, *refs):
    pieces, refs = refs[:-12], refs[-12:]
    query_ref, probs_ref, class_ref, kv_ref, middle_ref, normed_two_ref, front_out = refs[:7]
    packed_buf, tail_buf, tail_context, front_ref, sems = refs[7:]
    img = pl.program_id(1)
    at = pl.program_id(0) * IMGS_ROW + img
    lane = lax.broadcasted_iota(jnp.int32, (1, 128), 1)
    scale = HDIM ** (-0.5)
    halves = [
        jnp.where(lane < HDIM, scale, 0.0).astype(BF16),
        jnp.where(lane < HDIM, 0.0, scale).astype(BF16),
    ]

    kept = pltpu.make_async_copy(front_ref, front_out, sems.at[0])

    @pl.when(at == 0)
    def _():
        run_copies(plan(pieces, front_ref), sems)
        kept.start()

    @pl.when(at == pl.num_programs(0) * IMGS_ROW - 1)
    def _():
        kept.wait()

    @pl.when(img == 0)
    def _():
        ends = [normed_ref[0, end - 16 : end, :] for end in range(BLOCK, ROW + 1, BLOCK)]
        tail_buf[...] = dot(jnp.concatenate(ends, axis=0), front_ref[:, : 3 * D]).astype(BF16)
        tail_at = lax.broadcasted_iota(jnp.int32, (1, 16 * IMGS_ROW), 1)
        tail_bias = jnp.where(tail_at % 16 >= 16 - TAIL, 0.0, MASKED_SCORE)
        tail_ones = jnp.ones((16 * IMGS_ROW, 128), BF16)
        for pair in range(HEADS // 2):
            q, k, v = (tail_buf[:, part * D + pair * 128 : part * D + (pair + 1) * 128] for part in range(3))
            tail_context[:, pair * 128 : (pair + 1) * 128] = softmax_pair(
                q, k, jnp.concatenate([v, tail_ones], axis=1), tail_bias, halves
            )

    tokens = normed_ref[0, pl.ds(pl.multiple_of(img * BLOCK, BLOCK), BLOCK), :]
    for part in range(3):
        cols = slice(part * D, (part + 1) * D)
        packed_buf[:, cols] = dot(tokens, front_ref[:, cols]).astype(BF16)
    kv_ref[0] = packed_buf[:, D:]
    query_ref[at] = packed_buf[:16, :D]
    key_at = lax.broadcasted_iota(jnp.int32, (1, BLOCK), 1)
    bias = jnp.where(key_at < IMG, 0.0, MASKED_SCORE)
    queries = packed_buf[0:1, :D] * head_rows_mask().astype(BF16) * np.float32(scale).astype(BF16)
    scores = dot_t(queries, packed_buf[:, D : 2 * D]) + bias
    probs = jnp.exp(scores - jnp.max(scores, axis=-1, keepdims=True))
    probs_ref[at] = probs / jnp.sum(probs, axis=-1, keepdims=True)
    ones = jnp.ones((BLOCK, 128), BF16)
    is_tail = lax.broadcasted_iota(jnp.int32, (16, D), 0) >= 16 - TAIL
    context = []
    for pair in range(HEADS // 2):
        q, k, v = (packed_buf[:, part * D + pair * 128 : part * D + (pair + 1) * 128] for part in range(3))
        context.append(softmax_pair(q, k, jnp.concatenate([v, ones], axis=1), bias, halves))
    context = jnp.concatenate(context, axis=1)
    tail = tail_context[pl.ds(pl.multiple_of(img * 16, 16), 16), :]
    last = jnp.where(is_tail, tail, context[BLOCK - 16 :])
    context = jnp.concatenate([context[: BLOCK - 16], last], axis=0).astype(BF16)
    middle = resid_ref[0].astype(F32) + dot(context, front_ref[:, 3 * D :])
    middle_ref[...] = middle
    class_ref[at] = middle[:8]
    normed_two_ref[...] = (unit_norm(middle)[0] * gain_ref[...]).astype(BF16)


def head_rows_mask():
    return (
        lax.broadcasted_iota(jnp.int32, (HEADS_PAD, D), 1) // HDIM
        == lax.broadcasted_iota(jnp.int32, (HEADS_PAD, D), 0)
    ).astype(F32)


def attend(normed, resid, gain, pieces, plan, copies_n):
    rows_n = normed.shape[0]
    images = rows_n * IMGS_ROW
    near = pl.BlockSpec(memory_space=pltpu.VMEM)
    flat = pl.BlockSpec((BLOCK, D), lambda r, i: (r * IMGS_ROW + i, 0))
    return pl.pallas_call(
        functools.partial(attend_kernel, plan),
        grid=(rows_n, IMGS_ROW),
        in_specs=[
            pl.BlockSpec((1, ROW, D), lambda r, i: (r, 0, 0)),
            pl.BlockSpec((1, BLOCK, D), lambda r, i: (r, i, 0)),
            whole(gain),
        ]
        + [pl.BlockSpec(memory_space=pltpu.HBM)] * len(pieces),
        out_specs=[near] * 3
        + [
            pl.BlockSpec((1, BLOCK, 2 * D), lambda r, i: (r * IMGS_ROW + i, 0, 0)),
            flat,
            flat,
            pl.BlockSpec(memory_space=pltpu.HBM),
        ],
        out_shape=[
            pltpu.VMEM((images, 16, D), BF16),
            pltpu.VMEM((images, HEADS_PAD, BLOCK), F32),
            pltpu.VMEM((images, 8, D), F32),
            pltpu.HBM((images, BLOCK, 2 * D), BF16),
            pltpu.HBM((rows_n * ROW, D), F32),
            pltpu.HBM((rows_n * ROW, D), BF16),
            pltpu.HBM((D, 4 * D), BF16),
        ],
        scratch_shapes=[
            pltpu.VMEM((BLOCK, 3 * D), BF16),
            pltpu.VMEM((16 * IMGS_ROW, 3 * D), BF16),
            pltpu.VMEM((16 * IMGS_ROW, D), F32),
            pltpu.VMEM((D, 4 * D), BF16),
            pltpu.SemaphoreType.DMA((copies_n,)),
        ],
        compiler_params=params(24),
        cost_estimate=cost(8 * rows_n, 15 * rows_n),
        name="attend",
    )(far(normed), far(resid), gain, *pieces)


def class_kernel(
    plans, ids_ref, grads_ref, heads_ref, mlp_gain_ref, final_gain_ref,
    queries_ref, probs_ref, middles_ref, kv_hbm, front_hbm, *refs,
):
    feed_refs = refs[:-17]
    (
        sent_ref, weights_ref, routes_ref, d_class_ref, d_middle_ref, up_ref, down_ref,
        q_buf, c_buf, dq_buf, score_slots, prob_slots, kv_ref, front_ref, sems, up_sems, down_sems,
    ) = refs[-17:]
    images = middles_ref.shape[0]
    up_copies = start_copies(plans[0](feed_refs, up_ref), up_sems)
    down_copies = start_copies(plans[1](feed_refs, down_ref), down_sems)
    front_copy, kv_copy = start_copies([(front_hbm, front_ref), (kv_hbm, kv_ref)], sems)
    spread = (
        lax.broadcasted_iota(jnp.int32, (128, CLASSES * TASKS), 1) // TASKS
        == lax.broadcasted_iota(jnp.int32, (128, CLASSES * TASKS), 0)
    ).astype(F32).astype(BF16)
    task_at = lax.broadcasted_iota(jnp.int32, (images, CLASSES * TASKS), 1) % TASKS
    chosen = jnp.where(ids_ref[...] == task_at, dot(grads_ref[...], spread), 0.0).astype(BF16)
    d_final = dot(chosen, heads_ref[...])
    mlp_gain, final_gain = mlp_gain_ref[...], final_gain_ref[...]
    middle = middles_ref[:, 0, :]
    unit_mlp, inv_mlp = unit_norm(middle)
    for copy in up_copies:
        copy.wait()
    pre = dot((unit_mlp * mlp_gain).astype(BF16), up_ref[...])
    activated = gelu(pre).astype(BF16)
    for copy in down_copies:
        copy.wait()
    output = middle + dot(activated, down_ref[...])
    unit_fin, inv_fin = unit_norm(output)
    sent_ref[:, 2 * D : 3 * D] = (unit_fin * final_gain).astype(BF16)
    d_output = norm_back(d_final, unit_fin, inv_fin, final_gain)
    d_act = dot_t(d_output.astype(BF16), down_ref[...])
    d_pre = (d_act * gelu_slope(pre)).astype(BF16)
    d_middle = d_output + norm_back(dot_t(d_pre, up_ref[...]), unit_mlp, inv_mlp, mlp_gain)
    d_middle_ref[...] = d_middle
    front_copy.wait()
    d_context = dot_t(d_middle.astype(BF16), front_ref[:, 3 * D :]).astype(BF16)
    sent_ref[:, 3 * D : 4 * D] = d_context
    of_head = head_rows_mask()
    own = of_head.astype(BF16)
    scale = HDIM ** (-0.5)
    kv_copy.wait()
    for img in range(images):
        at = slice(img * HEADS_PAD, (img + 1) * HEADS_PAD)
        query = queries_ref[img, 0:1, :]
        sent_ref[img : img + 1, :D] = query
        q_buf[at] = query * own * np.float32(scale).astype(BF16)
        d_rows = d_context[img : img + 1] * own
        c_buf[at] = d_rows
        keys, values = kv_ref[img, :, :D], kv_ref[img, :, D:]
        probs = probs_ref[img]
        d_probs = dot_t(d_rows, values)
        d_scores = probs * (d_probs - jnp.sum(probs * d_probs, axis=-1, keepdims=True))
        score_slots[at] = d_scores[:, :128]
        prob_slots[at] = probs[:, :128]
        d_scores = d_scores.astype(BF16)
        weights_ref[img, :HEADS_PAD] = d_scores
        weights_ref[img, HEADS_PAD:] = probs.astype(BF16)
        dq_buf[img : img + 1] = jnp.sum(dot(d_scores, keys) * of_head, axis=0, keepdims=True) * scale
    lane = lax.broadcasted_iota(jnp.int32, (images, 128), 1)
    for slots, start in ((prob_slots, D), (score_slots, 4 * D)):
        for pair in range(HEADS // 2):
            first, second = (slots[pl.ds(2 * pair + h, images, stride=HEADS_PAD)] for h in range(2))
            both = jnp.where(lane < SLOTS, first, pltpu.roll(second, SLOTS, 1))
            sent_ref[:, start + pair * 128 : start + (pair + 1) * 128] = both.astype(BF16)
    sent_ref[:, 5 * D :] = grads_ref[...]
    by_key = dot_t(q_buf[...], front_ref[:, D : 2 * D]).astype(BF16)
    by_value = dot_t(c_buf[...], front_ref[:, 2 * D : 3 * D]).astype(BF16)
    for img in range(images):
        at = slice(img * HEADS_PAD, (img + 1) * HEADS_PAD)
        routes_ref[img, :HEADS_PAD] = by_key[at]
        routes_ref[img, HEADS_PAD:] = by_value[at]
    d_class_ref[...] = dot_t(dq_buf[...].astype(BF16), front_ref[:, :D])


SENT = 5 * D + 128


def class_path(ids, grads, heads, gains, attended, feed_weights):
    images = ids.shape[0]
    *small, kv, front = attended
    operands = (ids, grads, heads, *gains[1:], *small)
    feed_arrays, plans, copies_n = feed_weights
    remote = (far(kv), far(front), *feed_arrays)
    outs = [
        jax.ShapeDtypeStruct((images, SENT), BF16),
        jax.ShapeDtypeStruct((images, 2 * HEADS_PAD, BLOCK), BF16),
        jax.ShapeDtypeStruct((images, 2 * HEADS_PAD, D), BF16),
        jax.ShapeDtypeStruct((images, D), F32),
        jax.ShapeDtypeStruct((images, D), F32),
        pltpu.VMEM((D, FF), BF16),
        pltpu.VMEM((FF, D), BF16),
    ]
    near = pl.BlockSpec(memory_space=pltpu.VMEM)
    return pl.pallas_call(
        functools.partial(class_kernel, plans),
        in_specs=[near] * len(operands) + [pl.BlockSpec(memory_space=pltpu.HBM)] * len(remote),
        out_specs=[near] * len(outs),
        out_shape=outs,
        scratch_shapes=[
            pltpu.VMEM((images * HEADS_PAD, D), BF16),
            pltpu.VMEM((images * HEADS_PAD, D), BF16),
            pltpu.VMEM((images, D), F32),
            pltpu.VMEM((images * HEADS_PAD, 128), F32),
            pltpu.VMEM((images * HEADS_PAD, 128), F32),
            pltpu.VMEM(kv.shape, BF16),
            pltpu.VMEM((D, 4 * D), BF16),
            pltpu.SemaphoreType.DMA((2,)),
            pltpu.SemaphoreType.DMA((copies_n,)),
            pltpu.SemaphoreType.DMA((copies_n,)),
        ],
        compiler_params=params(24),
        cost_estimate=cost(8, 30),
        name="class_path",
    )(*operands, *remote)


FF_STEP = 768


def feed_kernel(normed_ref, middle_ref, up_ref, down_ref, *refs):
    out_ref, row_buf = refs[-2:]
    img = pl.program_id(0)
    rows = normed_ref[...]
    total = middle_ref[...]
    for step in range(FF // FF_STEP):
        at = slice(step * FF_STEP, (step + 1) * FF_STEP)
        total = total + dot(gelu(dot(rows, up_ref[:, at])).astype(BF16), down_ref[at, :])
    for at in range(IMGS_ROW):

        @pl.when(img == at)
        def _():
            row_buf[at * IMG : (at + 1) * IMG] = total[:IMG]
            row_buf[TAIL_AT + at * TAIL : TAIL_AT + (at + 1) * TAIL] = total[IMG:]

    @pl.when(img == IMGS_ROW - 1)
    def _():
        out_ref[0] = row_buf[...].astype(BF16)


def feed(normed, middle, up_all, down_all, row, rows_n, chain):
    spec = pl.BlockSpec((BLOCK, D), lambda i: (row * IMGS_ROW + i, 0))
    chained = [] if chain is None else [chain]
    return pl.pallas_call(
        feed_kernel,
        grid=(IMGS_ROW,),
        in_specs=[spec, spec]
        + [pl.BlockSpec(memory_space=pltpu.VMEM)] * 2
        + [pl.BlockSpec(memory_space=pltpu.HBM)] * len(chained),
        out_specs=pl.BlockSpec((1, ROW, D), lambda i: (row, 0, 0)),
        out_shape=pltpu.HBM((rows_n, ROW, D), BF16),
        input_output_aliases={} if chain is None else {4: 0},
        scratch_shapes=[pltpu.VMEM((ROW, D), F32)],
        compiler_params=params(18),
        cost_estimate=cost(10, 20),
        name="feed",
    )(far(normed), far(middle), up_all, down_all, *chained)


def token_grads_kernel(resid_ref, weights_ref, routes_ref, d_class_ref, d_middle_ref, gain_ref, out_ref):
    row_at = pl.program_id(0)
    gain = gain_ref[...]
    place = lax.broadcasted_iota(jnp.int32, (BLOCK, 1), 0)
    is_class = (place == 0).astype(F32)
    keep = jnp.where((place == 0) | (place > PROMPTS), 1.0, 0.0)
    for img in range(IMGS_ROW):
        one = pl.ds(row_at * IMGS_ROW + img, 1)
        unit_rows, inv_std = unit_norm(resid_ref[0, img * BLOCK : (img + 1) * BLOCK].astype(F32))
        d_normed = lax.dot_general(
            weights_ref[img], routes_ref[img], (((0,), (0,)), ((), ())), preferred_element_type=F32
        )
        d_normed = d_normed + is_class * d_class_ref[one]
        d_resid = norm_back(d_normed, unit_rows, inv_std, gain) + is_class * d_middle_ref[one]
        out_ref[0, img * IMG : (img + 1) * IMG] = (d_resid * keep)[:IMG]
    out_ref[0, TAIL_AT:] = jnp.zeros((ROW - TAIL_AT, D), F32)


def token_grads(resid, weights, routes, d_class, d_middle, gain):
    rows_n = resid.shape[0]
    row_spec = pl.BlockSpec((1, ROW, D), lambda r: (r, 0, 0))
    img_spec = lambda width: pl.BlockSpec((IMGS_ROW, 2 * HEADS_PAD, width), lambda r: (r, 0, 0))
    return pl.pallas_call(
        token_grads_kernel,
        grid=(rows_n,),
        in_specs=[row_spec, img_spec(BLOCK), img_spec(D), whole(d_class), whole(d_middle), whole(gain)],
        out_specs=row_spec,
        out_shape=pltpu.HBM(resid.shape, F32),
        compiler_params=params(20),
        cost_estimate=cost(0.5, 20),
        name="token_grads",
    )(far(resid), weights, routes, d_class, d_middle, gain)


def sums_kernel(front_ref, prompts_ref, gain_ref, *refs):
    parts, (prompt_out, head_out, all_buf, sum_buf, prompt_buf, sems) = refs[:-6], refs[-6:]
    rows = parts[0].shape[0]
    run_copies([(part, all_buf.at[pl.ds(at * rows, rows), :]) for at, part in enumerate(parts)], sems)
    scale = np.float32(HDIM ** (-0.5)).astype(BF16)
    column = lambda at: all_buf[:, at * D : (at + 1) * D]
    by_class = all_buf[:, 5 * D :].T
    ids = by_class[CLASSES : CLASSES + 1].astype(F32)
    masks = [(ids == task).astype(F32).astype(BF16) for task in range(TASKS)]
    of_task = (lax.broadcasted_iota(jnp.int32, (TASKS, 1), 0).astype(F32) == ids).astype(F32)
    spread = by_class[:CLASSES].astype(F32)[:, None, :] * of_task[None]
    head_out[...] = dot(spread.reshape(CLASSES * TASKS, -1).astype(BF16), column(2))
    lane = lax.broadcasted_iota(jnp.int32, (SLOTS, 128), 1)
    for side, (slots, lane_rows) in enumerate(((column(4), column(0) * scale), (column(1), column(3)))):
        slots = slots.T
        for pair in range(HEADS // 2):
            at = slice(pair * 128, (pair + 1) * 128)
            summed = dot(jnp.concatenate([slots[at] * mask for mask in masks], axis=0), lane_rows[:, at])
            for task in range(TASKS):
                first, second = (summed[task * 128 + h * SLOTS : task * 128 + (h + 1) * SLOTS] for h in range(2))
                sum_buf[task * SLOTS : (task + 1) * SLOTS, side * D + pair * 128 : side * D + (pair + 1) * 128] = (
                    jnp.where(lane < HDIM, first, second).astype(BF16)
                )
    d_normed = dot_t(sum_buf[...], front_ref[:, D : 3 * D])
    by_lanes(prompt_buf, prompts_ref[...].astype(F32))
    for task in range(TASKS):
        unit_rows, inv_std = unit_norm(read_strided(prompt_buf, task, PROMPTS))
        d_task = d_normed[task * SLOTS + 1 : task * SLOTS + 1 + PROMPTS]
        write_strided(prompt_buf, task, norm_back(d_task, unit_rows, inv_std, gain_ref[...]))
    for block, lanes in enumerate(LANE_BLOCKS):
        prompt_out[:, lanes] = prompt_buf[block]


def sums(front, prompts, gain, parts):
    operands = (front, prompts, gain)
    outs = [
        jax.ShapeDtypeStruct((PROMPTS * TASKS, D), F32),
        jax.ShapeDtypeStruct((CLASSES * TASKS, D), F32),
    ]
    images = sum(part.shape[0] for part in parts)
    return pl.pallas_call(
        sums_kernel,
        grid=(1,),
        in_specs=[pl.BlockSpec(memory_space=pltpu.VMEM)] * len(operands)
        + [pl.BlockSpec(memory_space=pl.ANY)] * len(parts),
        out_specs=[whole(o) for o in outs],
        out_shape=outs,
        scratch_shapes=[
            pltpu.VMEM((images, SENT), BF16),
            pltpu.VMEM((TASKS * SLOTS, 2 * D), BF16),
            pltpu.VMEM((len(LANE_BLOCKS), PROMPTS * TASKS, LANES), F32),
            pltpu.SemaphoreType.DMA((len(parts),)),
        ],
        compiler_params=params(28 if images <= 512 else 60),
        cost_estimate=cost(5, 15),
        name="sums",
    )(*operands, *parts)


def gather_rows(shard, dp):
    part = shard.shape[0] // dp
    mine = lax.dynamic_slice_in_dim(shard, lax.axis_index("dp") * part, part, 0)
    return lax.all_gather(mine, ("fsdp", "dp"), axis=0, tiled=True)


def copy_whole(at):
    return lambda refs, dst: [(refs[at], dst)]


def places():
    d, f = lax.axis_index("dp"), lax.axis_index("fsdp")
    return d // 2, d % 2, f // 2, f % 2


def exchange(value, dy=0, dc=0, dz=0, dx=0):
    pairs = []
    for at in range(32):
        y, c, z, x = at // 16, at // 8 % 2, at // 2 % 4, at % 2
        pairs.append((at, (((y ^ dy) * 2 + (c ^ dc)) * 4 + (z ^ dz)) * 2 + (x ^ dx)))
    return lax.ppermute(value, ("dp", "fsdp"), pairs)


HALF_COLS = 2 * D


class Fetch:
    def __init__(self, own, mine, both, cut):
        self.own, self.mine, self.both, self.cut, self.half = own, mine, both, cut, mine.shape[0]

    def along_z(self):
        self.column = jnp.concatenate([exchange(self.mine, dz=r) for r in (1, 2, 3)], axis=0)

    def beside(self):
        self.own_x = exchange(self.both, dx=1)

    def across(self):
        self.over_x = exchange(self.column, dx=1)
        self.over_y = exchange(self.column, dy=1)

    def diagonal(self):
        self.diag_y = exchange(self.over_x[: self.cut], dy=1)
        self.diag_x = exchange(self.over_y[self.cut :], dx=1)

    def pieces(self):
        near = [self.own_x, self.column, self.over_x, self.over_y, self.diag_y, self.diag_x]
        return self.own + near + [exchange(piece, dc=1) for piece in near]

    def plan(self, refs, dst, put):
        y, c, z, x = places()
        half, cut = self.half, self.cut
        pairs = []
        for side in range(2):
            own_x, column, over_x, over_y, diag_y, diag_x = refs[6 * side : 6 + 6 * side]

            def add(ref, start, count, r, x_at, y_at, within=0):
                return put(ref, start, count, dst, (z ^ r) * 2 + x_at, y_at, c ^ side, within)

            for y_at in range(2):
                pairs += add(own_x, y_at * half, half, 0, x ^ 1, y_at)
            for r in (1, 2, 3):
                start = (r - 1) * half
                pairs += add(column, start, half, r, x, y)
                pairs += add(over_x, start, half, r, x ^ 1, y)
                pairs += add(over_y, start, half, r, x, y ^ 1)
                first = min(max(cut - start, 0), half)
                if first:
                    pairs += add(diag_y, start, first, r, x ^ 1, y ^ 1)
                if first < half:
                    pairs += add(diag_x, start + first - cut, half - first, r, x ^ 1, y ^ 1, first)
        return pairs


def own_rows(ref, dst):
    _, _, z, x = places()
    count = ref.shape[0]
    return [(ref, dst.at[pl.ds(pl.multiple_of((z * 2 + x) * count, count), count), :])]


def put_front(ref, start, count, dst, place, y, c, within):
    row = pl.multiple_of(place * 96 + y * 48 + within, 16)
    cols = pl.ds(pl.multiple_of(c * HALF_COLS, 128), HALF_COLS)
    return [(ref.at[pl.ds(start, count), :], dst.at[pl.ds(row, count), cols])]


def front_bundle(shard):
    y, c, _, _ = places()
    mine = lax.dynamic_slice(shard, (y * 48, c * HALF_COLS), (48, HALF_COLS))
    both = lax.dynamic_slice(shard, (0, c * HALF_COLS), (96, HALF_COLS))
    return Fetch([shard], mine, both, 80)


def fetch_rest(up_shard, down_shard):
    d = lax.axis_index("dp")
    up_part = lax.dynamic_slice(up_shard, (0, d * D), (96, D))
    down_part = lax.dynamic_slice_in_dim(down_shard, d * 96, 96, 0)
    gathered = lax.all_gather(jnp.concatenate([up_part, down_part], axis=0), ("fsdp", "dp"), axis=0)
    gathered = gathered.reshape(8, 4, 192, D)

    def up_plan(refs, dst):
        dst = dst.reshape(8, 96, FF)
        return [(refs[0].at[:, d, 0:96, :], dst.at[:, :, D * d : D * d + D]) for d in range(4)]

    def down_plan(refs, dst):
        return [(refs[0].at[:, :, 96:192, :], dst.reshape(8, 4, 96, D))]

    return [far(gathered)], (up_plan, down_plan), 4


def share_rows(rows, works):
    done, parts = None, [rows]
    for work, shifts in zip(works, ([dict(dz=r) for r in (1, 2, 3)], [dict(dx=1)], [dict(dy=1)])):
        rows = jnp.concatenate(parts, axis=0) if len(parts) > 1 else rows
        if done is not None:
            rows, done = lax.optimization_barrier((rows, done))
        parts = [rows] + [exchange(rows, **shift) for shift in shifts]
        done = work(done)
    *parts, done = lax.optimization_barrier((*parts, done))
    return parts + [exchange(part, dc=1) for part in parts], done


def body(
    tuned, dp, tokens, task_ids, logit_grads, prompts, head_weights, qkv_weight, out_weight, up_weight, down_weight,
    attn_gain, mlp_gain, final_gain,
):
    rows_n = tokens.shape[0] * tokens.shape[1]
    images = rows_n * IMGS_ROW
    front_shard = jnp.concatenate([qkv_weight, out_weight], axis=1)
    gains = [gain.reshape(1, D) for gain in (attn_gain, mlp_gain, final_gain)]
    ids = task_ids.reshape(rows_n, IMGS_ROW)
    prompt_rows = prompts.transpose(1, 0, 2).reshape(PROMPTS * TASKS, D)
    resid, normed = assemble(ids, tokens.reshape(rows_n, ROW, D), prompt_rows, gains[0])
    token_rows = tokens.reshape(rows_n, ROW, D)
    ids_col = ids.reshape(images, 1)
    head_rows = head_weights.transpose(2, 0, 1).reshape(CLASSES * TASKS, D)
    grads = jnp.concatenate(
        [logit_grads.reshape(images, CLASSES), jnp.broadcast_to(ids_col, (images, 128 - CLASSES)).astype(BF16)], axis=1
    )
    tie = lambda *values: lax.optimization_barrier(values)
    if tuned:
        feed_weights = fetch_rest(up_weight, down_weight)
        front_in = front_bundle(front_shard)
        front_in.along_z()
        front_in.beside()
        resid, normed = assemble(ids, token_rows, prompt_rows, gains[0])
        front_in.column, normed = tie(front_in.column, normed)
        front_in.across()
        front_in.diagonal()
        plan_front = lambda refs, dst: own_rows(refs[0], dst) + front_in.plan(refs[1:], dst, put_front)
        fetched = [far(piece) for piece in front_in.pieces()], plan_front, 1 + 2 * (2 + 9 + 4)
    else:
        feed_weights = [gather_rows(w, dp) for w in (up_weight, down_weight)], (copy_whole(0), copy_whole(1)), 1
        resid, normed = assemble(ids, token_rows, prompt_rows, gains[0])
        fetched = [gather_rows(front_shard, dp)], copy_whole(0), 1
    *attended, middle, normed_two, front = attend(normed, resid, gains[1], *fetched)
    sent, weights, routes, d_class, d_middle, up_all, down_all = class_path(
        ids_col, grads, head_rows, gains, [*attended, front], feed_weights
    )

    def feed_rows(rows, chain):
        for row in rows:
            chain = feed(normed_two, middle, up_all, down_all, row, rows_n, chain)
        return chain

    works = (
        lambda done: (token_grads(resid, weights, routes, d_class, d_middle, gains[0]), None),
        lambda done: (done[0], feed_rows(range(rows_n // 2), None)),
        lambda done: (done[0], feed_rows(range(rows_n // 2, rows_n), done[1])),
    )
    if tuned:
        parts, (input_grads, activations) = share_rows(sent, works)
    else:
        parts = [lax.all_gather(sent, ("dp", "fsdp"), axis=0, tiled=True)]
        input_grads, activations = works[2](works[1](works[0](None)))
    prompt_out, head_out = sums(front, prompt_rows, gains[0], parts)
    return (
        activations.reshape(tokens.shape),
        input_grads.reshape(tokens.shape),
        prompt_out.reshape(PROMPTS, TASKS, D).transpose(1, 0, 2),
        head_out.reshape(CLASSES, TASKS, D).transpose(1, 2, 0),
    )


def solution(mesh):
    rows = P(None, ("dp", "fsdp"), None, None)
    in_specs = (rows, P(None, ("dp", "fsdp"), None), rows, P(), P(), *(P("fsdp", None),) * 4, P(), P(), P())
    return jax.shard_map(
        functools.partial(body, dict(mesh.shape) == {"dp": 4, "fsdp": 8}, mesh.shape["dp"]),
        mesh=mesh,
        in_specs=in_specs,
        out_specs=(rows, rows, P(), P()),
        check_vma=False,
    )
```

```python
import functools

import jax
import jax.numpy as jnp
import numpy as np
from jax import lax
from jax.experimental import pallas as pl
from jax.experimental.pallas import tpu as pltpu
from jax.sharding import PartitionSpec as P

D = 768
HEADS = 12
HDIM = 64
FF = 3072
CLASSES = 100
TASKS = 8
PROMPTS = 50
IMG = 247
IMGS_ROW = 4
ROW = 1024
MB = 2

BLOCK = 256
TAIL = BLOCK - IMG
TAIL_AT = IMGS_ROW * IMG
HEADS_PAD = 16
SLOTS = 64
EPSILON = 1e-06
MASKED_SCORE = -1e30
BF16 = jnp.bfloat16
F32 = jnp.float32


def dot(lhs, rhs):
    return lax.dot_general(lhs, rhs, (((1,), (0,)), ((), ())), preferred_element_type=F32)


def dot_t(lhs, rhs):
    return lax.dot_general(lhs, rhs, (((1,), (1,)), ((), ())), preferred_element_type=F32)


def unit_norm(rows):
    centred = rows - jnp.mean(rows, axis=-1, keepdims=True)
    inv_std = lax.rsqrt(jnp.mean(centred * centred, axis=-1, keepdims=True) + EPSILON)
    return centred * inv_std, inv_std


def norm_back(grad_out, unit_rows, inv_std, gain):
    scaled = grad_out * gain
    inner_mean = jnp.mean(scaled * unit_rows, axis=-1, keepdims=True)
    return inv_std * (scaled - jnp.mean(scaled, axis=-1, keepdims=True) - unit_rows * inner_mean)


def gelu(rows):
    return 0.5 * rows * (1.0 + lax.erf(rows * np.float32(np.sqrt(0.5))))


def gelu_slope(rows):
    upper = 0.5 * (1.0 + lax.erf(rows * np.float32(np.sqrt(0.5))))
    return upper + rows * jnp.exp(-0.5 * rows * rows) * np.float32(1.0 / np.sqrt(2.0 * np.pi))


def params(mib):
    return pltpu.CompilerParams(vmem_limit_bytes=mib << 20)


def cost(gflops, mbytes):
    return pl.CostEstimate(flops=int(gflops * 1e9), bytes_accessed=int(mbytes * 1e6), transcendentals=0)


def far(array):
    return pltpu.with_memory_space_constraint(array, pltpu.HBM)


def whole(array):
    return pl.BlockSpec(array.shape, lambda *grid: (0,) * array.ndim, pipeline_mode=pl.Buffered(1))


def make_copies(pairs, sems, first=0):
    return [pltpu.make_async_copy(src, dst, sems.at[first + k]) for k, (src, dst) in enumerate(pairs)]


def start_copies(pairs, sems):
    copies = make_copies(pairs, sems)
    for copy in copies:
        copy.start()
    return copies


def run_copies(pairs, sems):
    for copy in start_copies(pairs, sems):
        copy.wait()


LANES = 128
LANE_BLOCKS = [slice(at, at + LANES) for at in range(0, D, LANES)]


def by_lanes(buf, rows):
    for block, lanes in enumerate(LANE_BLOCKS):
        buf[block] = rows[:, lanes]


def read_strided(buf, start, count):
    at = pl.ds(start, count, stride=TASKS)
    return jnp.concatenate([buf[block, at] for block in range(len(LANE_BLOCKS))], axis=1)


def write_strided(buf, start, rows):
    at = pl.ds(start, rows.shape[0], stride=TASKS)
    for block, lanes in enumerate(LANE_BLOCKS):
        buf[block, at] = rows[:, lanes]


def assemble_kernel(
    ids_ref, tokens_ref, prompts_ref, gain_ref, resid_ref, normed_ref, row_buf, img_buf, prompt_buf
):
    row_at = pl.program_id(0)
    by_lanes(prompt_buf, prompts_ref[...].astype(F32))
    row_buf[...] = tokens_ref[0].astype(F32)
    for img in range(IMGS_ROW):
        img_buf[0 : IMG + 1] = row_buf[img * IMG : img * IMG + IMG + 1]
        img_buf[IMG:BLOCK] = row_buf[TAIL_AT + img * TAIL : TAIL_AT + (img + 1) * TAIL]
        img_buf[1 : 1 + PROMPTS] = read_strided(prompt_buf, ids_ref[row_at, img], PROMPTS)
        rows = img_buf[...]
        at = slice(img * BLOCK, (img + 1) * BLOCK)
        resid_ref[0, at] = rows.astype(BF16)
        unit_rows, _ = unit_norm(rows)
        normed_ref[0, at] = (unit_rows * gain_ref[...]).astype(BF16)


def assemble(ids, tokens, prompts, gain):
    rows_n = tokens.shape[0]
    row_spec = pl.BlockSpec((1, ROW, D), lambda r: (r, 0, 0))
    return pl.pallas_call(
        assemble_kernel,
        grid=(rows_n,),
        in_specs=[pl.BlockSpec(memory_space=pltpu.SMEM), row_spec, whole(prompts), whole(gain)],
        out_specs=[row_spec, row_spec],
        out_shape=[pltpu.HBM(tokens.shape, BF16)] * 2,
        scratch_shapes=[
            pltpu.VMEM((ROW, D), F32),
            pltpu.VMEM((BLOCK, D), F32),
            pltpu.VMEM((len(LANE_BLOCKS), PROMPTS * TASKS, LANES), F32),
        ],
        compiler_params=params(20),
        cost_estimate=cost(0.1, 10),
        name="assemble",
    )(ids, tokens, prompts, gain)


def softmax_pair(queries, keys, values_ext, bias, first_half):
    halves = []
    for scale_row in first_half:
        scores = dot_t(queries * scale_row, keys) + bias
        weights = jnp.exp(scores - jnp.max(scores, axis=-1, keepdims=True)).astype(BF16)
        summed = dot(weights, values_ext)
        halves.append(summed[:, :128] / summed[:, 128:])
    lanes = lax.broadcasted_iota(jnp.int32, halves[0].shape, 1)
    return jnp.where(lanes < HDIM, halves[0], halves[1])


def attend_kernel(plan, normed_ref, resid_ref, gain_ref, *refs):
    pieces, refs = refs[:-12], refs[-12:]
    query_ref, probs_ref, class_ref, kv_ref, middle_ref, normed_two_ref, front_out = refs[:7]
    packed_buf, tail_buf, tail_context, front_ref, sems = refs[7:]
    img = pl.program_id(1)
    at = pl.program_id(0) * IMGS_ROW + img
    lane = lax.broadcasted_iota(jnp.int32, (1, 128), 1)
    scale = HDIM ** (-0.5)
    halves = [
        jnp.where(lane < HDIM, scale, 0.0).astype(BF16),
        jnp.where(lane < HDIM, 0.0, scale).astype(BF16),
    ]

    kept = pltpu.make_async_copy(front_ref, front_out, sems.at[0])

    @pl.when(at == 0)
    def _():
        run_copies(plan(pieces, front_ref), sems)
        kept.start()

    @pl.when(at == pl.num_programs(0) * IMGS_ROW - 1)
    def _():
        kept.wait()

    @pl.when(img == 0)
    def _():
        ends = [normed_ref[0, end - 16 : end, :] for end in range(BLOCK, ROW + 1, BLOCK)]
        tail_buf[...] = dot(jnp.concatenate(ends, axis=0), front_ref[:, : 3 * D]).astype(BF16)
        tail_at = lax.broadcasted_iota(jnp.int32, (1, 16 * IMGS_ROW), 1)
        tail_bias = jnp.where(tail_at % 16 >= 16 - TAIL, 0.0, MASKED_SCORE)
        tail_ones = jnp.ones((16 * IMGS_ROW, 128), BF16)
        for pair in range(HEADS // 2):
            q, k, v = (tail_buf[:, part * D + pair * 128 : part * D + (pair + 1) * 128] for part in range(3))
            tail_context[:, pair * 128 : (pair + 1) * 128] = softmax_pair(
                q, k, jnp.concatenate([v, tail_ones], axis=1), tail_bias, halves
            )

    tokens = normed_ref[0, pl.ds(pl.multiple_of(img * BLOCK, BLOCK), BLOCK), :]
    for part in range(3):
        cols = slice(part * D, (part + 1) * D)
        packed_buf[:, cols] = dot(tokens, front_ref[:, cols]).astype(BF16)
    kv_ref[0] = packed_buf[:, D:]
    query_ref[at] = packed_buf[:16, :D]
    key_at = lax.broadcasted_iota(jnp.int32, (1, BLOCK), 1)
    bias = jnp.where(key_at < IMG, 0.0, MASKED_SCORE)
    queries = packed_buf[0:1, :D] * head_rows_mask().astype(BF16) * np.float32(scale).astype(BF16)
    scores = dot_t(queries, packed_buf[:, D : 2 * D]) + bias
    probs = jnp.exp(scores - jnp.max(scores, axis=-1, keepdims=True))
    probs_ref[at] = probs / jnp.sum(probs, axis=-1, keepdims=True)
    ones = jnp.ones((BLOCK, 128), BF16)
    is_tail = lax.broadcasted_iota(jnp.int32, (16, D), 0) >= 16 - TAIL
    context = []
    for pair in range(HEADS // 2):
        q, k, v = (packed_buf[:, part * D + pair * 128 : part * D + (pair + 1) * 128] for part in range(3))
        context.append(softmax_pair(q, k, jnp.concatenate([v, ones], axis=1), bias, halves))
    context = jnp.concatenate(context, axis=1)
    tail = tail_context[pl.ds(pl.multiple_of(img * 16, 16), 16), :]
    last = jnp.where(is_tail, tail, context[BLOCK - 16 :])
    context = jnp.concatenate([context[: BLOCK - 16], last], axis=0).astype(BF16)
    middle = resid_ref[0].astype(F32) + dot(context, front_ref[:, 3 * D :])
    middle_ref[...] = middle
    class_ref[at] = middle[:8]
    normed_two_ref[...] = (unit_norm(middle)[0] * gain_ref[...]).astype(BF16)


def head_rows_mask():
    return (
        lax.broadcasted_iota(jnp.int32, (HEADS_PAD, D), 1) // HDIM
        == lax.broadcasted_iota(jnp.int32, (HEADS_PAD, D), 0)
    ).astype(F32)


def attend(normed, resid, gain, pieces, plan, copies_n):
    rows_n = normed.shape[0]
    images = rows_n * IMGS_ROW
    near = pl.BlockSpec(memory_space=pltpu.VMEM)
    flat = pl.BlockSpec((BLOCK, D), lambda r, i: (r * IMGS_ROW + i, 0))
    return pl.pallas_call(
        functools.partial(attend_kernel, plan),
        grid=(rows_n, IMGS_ROW),
        in_specs=[
            pl.BlockSpec((1, ROW, D), lambda r, i: (r, 0, 0)),
            pl.BlockSpec((1, BLOCK, D), lambda r, i: (r, i, 0)),
            whole(gain),
        ]
        + [pl.BlockSpec(memory_space=pltpu.HBM)] * len(pieces),
        out_specs=[near] * 3
        + [
            pl.BlockSpec((1, BLOCK, 2 * D), lambda r, i: (r * IMGS_ROW + i, 0, 0)),
            flat,
            flat,
            pl.BlockSpec(memory_space=pltpu.HBM),
        ],
        out_shape=[
            pltpu.VMEM((images, 16, D), BF16),
            pltpu.VMEM((images, HEADS_PAD, BLOCK), F32),
            pltpu.VMEM((images, 8, D), F32),
            pltpu.HBM((images, BLOCK, 2 * D), BF16),
            pltpu.HBM((rows_n * ROW, D), F32),
            pltpu.HBM((rows_n * ROW, D), BF16),
            pltpu.HBM((D, 4 * D), BF16),
        ],
        scratch_shapes=[
            pltpu.VMEM((BLOCK, 3 * D), BF16),
            pltpu.VMEM((16 * IMGS_ROW, 3 * D), BF16),
            pltpu.VMEM((16 * IMGS_ROW, D), F32),
            pltpu.VMEM((D, 4 * D), BF16),
            pltpu.SemaphoreType.DMA((copies_n,)),
        ],
        compiler_params=params(24),
        cost_estimate=cost(8 * rows_n, 15 * rows_n),
        name="attend",
    )(far(normed), far(resid), gain, *pieces)


def loss_kernel(ids_ref, grads_ref, heads_ref, d_final_ref):
    images = ids_ref.shape[0]
    spread = (
        lax.broadcasted_iota(jnp.int32, (128, CLASSES * TASKS), 1) // TASKS
        == lax.broadcasted_iota(jnp.int32, (128, CLASSES * TASKS), 0)
    ).astype(F32).astype(BF16)
    task_at = lax.broadcasted_iota(jnp.int32, (images, CLASSES * TASKS), 1) % TASKS
    chosen = jnp.where(ids_ref[...] == task_at, dot(grads_ref[...], spread), 0.0).astype(BF16)
    d_final_ref[...] = dot(chosen, heads_ref[...])


def loss_grads(ids, grads, heads):
    operands = (ids, grads, heads)
    out = jax.ShapeDtypeStruct((ids.shape[0], D), F32)
    return pl.pallas_call(
        loss_kernel,
        grid=(1,),
        in_specs=[whole(o) for o in operands],
        out_specs=whole(out),
        out_shape=out,
        compiler_params=params(12),
        cost_estimate=cost(0.1, 2),
        name="loss_grads",
    )(*operands)


def class_kernel(
    plans, d_final_ref, grads_ref, mlp_gain_ref, final_gain_ref,
    queries_ref, probs_ref, middles_ref, kv_hbm, front_hbm, *refs,
):
    feed_refs = refs[:-14]
    (
        sent_ref, weights_ref, routes_ref, d_class_ref, d_middle_ref, up_ref, down_ref,
        score_slots, prob_slots, kv_ref, front_ref, sems, up_sems, down_sems,
    ) = refs[-14:]
    images = middles_ref.shape[0]
    up_copies = make_copies(plans[0](feed_refs, up_ref), up_sems)
    down_copies = make_copies(plans[1](feed_refs, down_ref), down_sems)
    for pair in zip(up_copies, down_copies):
        for copy in pair:
            copy.start()
    front_copy, kv_copy = start_copies([(front_hbm, front_ref), (kv_hbm, kv_ref)], sems)
    mlp_gain, final_gain = mlp_gain_ref[...], final_gain_ref[...]
    middle = middles_ref[:, 0, :]
    unit_mlp, inv_mlp = unit_norm(middle)
    normed = (unit_mlp * mlp_gain).astype(BF16)
    output, pre = middle, []
    width = FF // len(up_copies)
    for at, (up_copy, down_copy) in enumerate(zip(up_copies, down_copies)):
        cols = slice(at * width, (at + 1) * width)
        up_copy.wait()
        pre.append(dot(normed, up_ref[:, cols]))
        down_copy.wait()
        output = output + dot(gelu(pre[-1]).astype(BF16), down_ref[cols, :])
    pre = jnp.concatenate(pre, axis=1)
    unit_fin, inv_fin = unit_norm(output)
    sent_ref[:, 2 * D : 3 * D] = (unit_fin * final_gain).astype(BF16)
    d_output = norm_back(d_final_ref[...], unit_fin, inv_fin, final_gain)
    d_act = dot_t(d_output.astype(BF16), down_ref[...])
    d_pre = (d_act * gelu_slope(pre)).astype(BF16)
    d_middle = d_output + norm_back(dot_t(d_pre, up_ref[...]), unit_mlp, inv_mlp, mlp_gain)
    d_middle_ref[...] = d_middle
    front_copy.wait()
    d_context = dot_t(d_middle.astype(BF16), front_ref[:, 3 * D :]).astype(BF16)
    sent_ref[:, 3 * D : 4 * D] = d_context
    of_head = head_rows_mask()
    scale = HDIM ** (-0.5)
    kv_copy.wait()
    queries = jnp.concatenate([queries_ref[img, 0:1, :] for img in range(images)], axis=0)
    sent_ref[:, :D] = queries
    spread_heads = lambda rows: (rows[:, None, :] * of_head[None]).reshape(images * HEADS_PAD, D).astype(BF16)
    by_head = spread_heads(d_context.astype(F32))
    probs = probs_ref[...].reshape(images * HEADS_PAD, BLOCK)
    rows_of = lambda array, img: array[img * HEADS_PAD : (img + 1) * HEADS_PAD]
    d_probs = jnp.concatenate(
        [dot_t(rows_of(by_head, img), kv_ref[img, :, D:]) for img in range(images)], axis=0
    )
    d_scores = probs * (d_probs - jnp.sum(probs * d_probs, axis=-1, keepdims=True))
    score_slots[...] = d_scores[:, :128]
    prob_slots[...] = probs[:, :128]
    d_scores = d_scores.astype(BF16)
    weights_ref[:, :HEADS_PAD] = d_scores.reshape(images, HEADS_PAD, BLOCK)
    weights_ref[:, HEADS_PAD:] = probs.astype(BF16).reshape(images, HEADS_PAD, BLOCK)
    d_queries = jnp.concatenate(
        [
            jnp.sum(dot(rows_of(d_scores, img), kv_ref[img, :, :D]) * of_head, axis=0, keepdims=True)
            for img in range(images)
        ],
        axis=0,
    )
    lane = lax.broadcasted_iota(jnp.int32, (images, 128), 1)
    for slots, start in ((prob_slots, D), (score_slots, 4 * D)):
        for pair in range(HEADS // 2):
            first, second = (slots[pl.ds(2 * pair + h, images, stride=HEADS_PAD)] for h in range(2))
            both = jnp.where(lane < SLOTS, first, pltpu.roll(second, SLOTS, 1))
            sent_ref[:, start + pair * 128 : start + (pair + 1) * 128] = both.astype(BF16)
    sent_ref[:, 5 * D :] = grads_ref[...]
    by_key = dot_t(spread_heads(queries.astype(F32) * scale), front_ref[:, D : 2 * D]).astype(BF16)
    by_value = dot_t(by_head, front_ref[:, 2 * D : 3 * D]).astype(BF16)
    routes_ref[:, :HEADS_PAD] = by_key.reshape(images, HEADS_PAD, D)
    routes_ref[:, HEADS_PAD:] = by_value.reshape(images, HEADS_PAD, D)
    d_class_ref[...] = dot_t((d_queries * scale).astype(BF16), front_ref[:, :D])


SENT = 5 * D + 128


def class_path(d_final, grads, gains, attended, feed_weights):
    images = d_final.shape[0]
    *small, kv, front = attended
    operands = (d_final, grads, *gains[1:], *small)
    feed_arrays, plans, copies_n = feed_weights
    remote = (far(kv), far(front), *feed_arrays)
    outs = [
        jax.ShapeDtypeStruct((images, SENT), BF16),
        jax.ShapeDtypeStruct((images, 2 * HEADS_PAD, BLOCK), BF16),
        jax.ShapeDtypeStruct((images, 2 * HEADS_PAD, D), BF16),
        jax.ShapeDtypeStruct((images, D), F32),
        jax.ShapeDtypeStruct((images, D), F32),
        pltpu.VMEM((D, FF), BF16),
        pltpu.VMEM((FF, D), BF16),
    ]
    near = pl.BlockSpec(memory_space=pltpu.VMEM)
    return pl.pallas_call(
        functools.partial(class_kernel, plans),
        in_specs=[near] * len(operands) + [pl.BlockSpec(memory_space=pltpu.HBM)] * len(remote),
        out_specs=[near] * len(outs),
        out_shape=outs,
        scratch_shapes=[
            pltpu.VMEM((images * HEADS_PAD, 128), F32),
            pltpu.VMEM((images * HEADS_PAD, 128), F32),
            pltpu.VMEM(kv.shape, BF16),
            pltpu.VMEM((D, 4 * D), BF16),
            pltpu.SemaphoreType.DMA((2,)),
            pltpu.SemaphoreType.DMA((copies_n,)),
            pltpu.SemaphoreType.DMA((copies_n,)),
        ],
        compiler_params=params(24),
        cost_estimate=cost(8, 30),
        name="class_path",
    )(*operands, *remote)


FF_STEP = 768


def feed_kernel(normed_ref, middle_ref, up_ref, down_ref, *refs):
    out_ref, row_buf = refs[-2:]
    img = pl.program_id(0)
    rows = normed_ref[...]
    total = middle_ref[...]
    for step in range(FF // FF_STEP):
        at = slice(step * FF_STEP, (step + 1) * FF_STEP)
        total = total + dot(gelu(dot(rows, up_ref[:, at])).astype(BF16), down_ref[at, :])
    for at in range(IMGS_ROW):

        @pl.when(img == at)
        def _():
            row_buf[at * IMG : (at + 1) * IMG] = total[:IMG]
            row_buf[TAIL_AT + at * TAIL : TAIL_AT + (at + 1) * TAIL] = total[IMG:]

    @pl.when(img == IMGS_ROW - 1)
    def _():
        out_ref[0] = row_buf[...].astype(BF16)


def feed(normed, middle, up_all, down_all, row, rows_n, chain):
    spec = pl.BlockSpec((BLOCK, D), lambda i: (row * IMGS_ROW + i, 0))
    chained = [] if chain is None else [chain]
    return pl.pallas_call(
        feed_kernel,
        grid=(IMGS_ROW,),
        in_specs=[spec, spec]
        + [pl.BlockSpec(memory_space=pltpu.VMEM)] * 2
        + [pl.BlockSpec(memory_space=pltpu.HBM)] * len(chained),
        out_specs=pl.BlockSpec((1, ROW, D), lambda i: (row, 0, 0)),
        out_shape=pltpu.HBM((rows_n, ROW, D), BF16),
        input_output_aliases={} if chain is None else {4: 0},
        scratch_shapes=[pltpu.VMEM((ROW, D), F32)],
        compiler_params=params(18),
        cost_estimate=cost(10, 20),
        name="feed",
    )(far(normed), far(middle), up_all, down_all, *chained)


def token_grads_kernel(resid_ref, weights_ref, routes_ref, d_class_ref, d_middle_ref, gain_ref, out_ref):
    row_at = pl.program_id(0)
    gain = gain_ref[...]
    place = lax.broadcasted_iota(jnp.int32, (BLOCK, 1), 0)
    is_class = (place == 0).astype(F32)
    keep = jnp.where((place == 0) | (place > PROMPTS), 1.0, 0.0)
    for img in range(IMGS_ROW):
        one = pl.ds(row_at * IMGS_ROW + img, 1)
        unit_rows, inv_std = unit_norm(resid_ref[0, img * BLOCK : (img + 1) * BLOCK].astype(F32))
        d_normed = lax.dot_general(
            weights_ref[img], routes_ref[img], (((0,), (0,)), ((), ())), preferred_element_type=F32
        )
        d_normed = d_normed + is_class * d_class_ref[one]
        d_resid = norm_back(d_normed, unit_rows, inv_std, gain) + is_class * d_middle_ref[one]
        out_ref[0, img * IMG : (img + 1) * IMG] = (d_resid * keep)[:IMG]
    out_ref[0, TAIL_AT:] = jnp.zeros((ROW - TAIL_AT, D), F32)


def token_grads(resid, weights, routes, d_class, d_middle, gain):
    rows_n = resid.shape[0]
    row_spec = pl.BlockSpec((1, ROW, D), lambda r: (r, 0, 0))
    img_spec = lambda width: pl.BlockSpec((IMGS_ROW, 2 * HEADS_PAD, width), lambda r: (r, 0, 0))
    return pl.pallas_call(
        token_grads_kernel,
        grid=(rows_n,),
        in_specs=[row_spec, img_spec(BLOCK), img_spec(D), whole(d_class), whole(d_middle), whole(gain)],
        out_specs=row_spec,
        out_shape=pltpu.HBM(resid.shape, F32),
        compiler_params=params(20),
        cost_estimate=cost(0.5, 20),
        name="token_grads",
    )(far(resid), weights, routes, d_class, d_middle, gain)


def sums_kernel(front_ref, prompts_ref, gain_ref, *refs):
    parts, (prompt_out, head_out, all_buf, sum_buf, prompt_buf, sems) = refs[:-6], refs[-6:]
    rows = parts[0].shape[0]
    run_copies([(part, all_buf.at[pl.ds(at * rows, rows), :]) for at, part in enumerate(parts)], sems)
    scale = np.float32(HDIM ** (-0.5)).astype(BF16)
    column = lambda at: all_buf[:, at * D : (at + 1) * D]
    by_class = all_buf[:, 5 * D :].T
    ids = by_class[CLASSES : CLASSES + 1].astype(F32)
    masks = [(ids == task).astype(F32).astype(BF16) for task in range(TASKS)]
    of_task = (lax.broadcasted_iota(jnp.int32, (TASKS, 1), 0).astype(F32) == ids).astype(F32)
    spread = by_class[:CLASSES].astype(F32)[:, None, :] * of_task[None]
    head_out[...] = dot(spread.reshape(CLASSES * TASKS, -1).astype(BF16), column(2))
    lane = lax.broadcasted_iota(jnp.int32, (SLOTS, 128), 1)
    for side, (slots, lane_rows) in enumerate(((column(4), column(0) * scale), (column(1), column(3)))):
        slots = slots.T
        for pair in range(HEADS // 2):
            at = slice(pair * 128, (pair + 1) * 128)
            summed = dot(jnp.concatenate([slots[at] * mask for mask in masks], axis=0), lane_rows[:, at])
            for task in range(TASKS):
                first, second = (summed[task * 128 + h * SLOTS : task * 128 + (h + 1) * SLOTS] for h in range(2))
                sum_buf[task * SLOTS : (task + 1) * SLOTS, side * D + pair * 128 : side * D + (pair + 1) * 128] = (
                    jnp.where(lane < HDIM, first, second).astype(BF16)
                )
    d_normed = dot_t(sum_buf[...], front_ref[:, D : 3 * D])
    by_lanes(prompt_buf, prompts_ref[...].astype(F32))
    for task in range(TASKS):
        unit_rows, inv_std = unit_norm(read_strided(prompt_buf, task, PROMPTS))
        d_task = d_normed[task * SLOTS + 1 : task * SLOTS + 1 + PROMPTS]
        write_strided(prompt_buf, task, norm_back(d_task, unit_rows, inv_std, gain_ref[...]))
    for block, lanes in enumerate(LANE_BLOCKS):
        prompt_out[:, lanes] = prompt_buf[block]


def sums(front, prompts, gain, parts):
    operands = (front, prompts, gain)
    outs = [
        jax.ShapeDtypeStruct((PROMPTS * TASKS, D), F32),
        jax.ShapeDtypeStruct((CLASSES * TASKS, D), F32),
    ]
    images = sum(part.shape[0] for part in parts)
    return pl.pallas_call(
        sums_kernel,
        grid=(1,),
        in_specs=[pl.BlockSpec(memory_space=pltpu.VMEM)] * len(operands)
        + [pl.BlockSpec(memory_space=pl.ANY)] * len(parts),
        out_specs=[whole(o) for o in outs],
        out_shape=outs,
        scratch_shapes=[
            pltpu.VMEM((images, SENT), BF16),
            pltpu.VMEM((TASKS * SLOTS, 2 * D), BF16),
            pltpu.VMEM((len(LANE_BLOCKS), PROMPTS * TASKS, LANES), F32),
            pltpu.SemaphoreType.DMA((len(parts),)),
        ],
        compiler_params=params(28 if images <= 512 else 60),
        cost_estimate=cost(5, 15),
        name="sums",
    )(*operands, *parts)


def gather_rows(shard, dp):
    part = shard.shape[0] // dp
    mine = lax.dynamic_slice_in_dim(shard, lax.axis_index("dp") * part, part, 0)
    return lax.all_gather(mine, ("fsdp", "dp"), axis=0, tiled=True)


def copy_whole(at):
    return lambda refs, dst: [(refs[at], dst)]


def places():
    d, f = lax.axis_index("dp"), lax.axis_index("fsdp")
    return d // 2, d % 2, f // 2, f % 2


def exchange(value, dy=0, dc=0, dz=0, dx=0):
    pairs = []
    for at in range(32):
        y, c, z, x = at // 16, at // 8 % 2, at // 2 % 4, at % 2
        pairs.append((at, (((y ^ dy) * 2 + (c ^ dc)) * 4 + (z ^ dz)) * 2 + (x ^ dx)))
    return lax.ppermute(value, ("dp", "fsdp"), pairs)


HALF_COLS = 2 * D


class Fetch:
    def __init__(self, own, mine, both, cut):
        self.own, self.mine, self.both, self.cut, self.half = own, mine, both, cut, mine.shape[0]

    def along_z(self):
        self.column = jnp.concatenate([exchange(self.mine, dz=r) for r in (1, 2, 3)], axis=0)

    def beside(self):
        self.own_x = exchange(self.both, dx=1)

    def across(self):
        self.over_x = exchange(self.column, dx=1)
        self.over_y = exchange(self.column, dy=1)

    def diagonal(self):
        self.diag_y = exchange(self.over_x[: self.cut], dy=1)
        self.diag_x = exchange(self.over_y[self.cut :], dx=1)

    def pieces(self):
        near = [self.own_x, self.column, self.over_x, self.over_y, self.diag_y, self.diag_x]
        return self.own + near + [exchange(piece, dc=1) for piece in near]

    def plan(self, refs, dst, put):
        y, c, z, x = places()
        half, cut = self.half, self.cut
        pairs = []
        for side in range(2):
            own_x, column, over_x, over_y, diag_y, diag_x = refs[6 * side : 6 + 6 * side]

            def add(ref, start, count, r, x_at, y_at, within=0):
                return put(ref, start, count, dst, (z ^ r) * 2 + x_at, y_at, c ^ side, within)

            for y_at in range(2):
                pairs += add(own_x, y_at * half, half, 0, x ^ 1, y_at)
            for r in (1, 2, 3):
                start = (r - 1) * half
                pairs += add(column, start, half, r, x, y)
                pairs += add(over_x, start, half, r, x ^ 1, y)
                pairs += add(over_y, start, half, r, x, y ^ 1)
                first = min(max(cut - start, 0), half)
                if first:
                    pairs += add(diag_y, start, first, r, x ^ 1, y ^ 1)
                if first < half:
                    pairs += add(diag_x, start + first - cut, half - first, r, x ^ 1, y ^ 1, first)
        return pairs


def own_rows(ref, dst):
    _, _, z, x = places()
    count = ref.shape[0]
    return [(ref, dst.at[pl.ds(pl.multiple_of((z * 2 + x) * count, count), count), :])]


def put_front(ref, start, count, dst, place, y, c, within):
    row = pl.multiple_of(place * 96 + y * 48 + within, 16)
    cols = pl.ds(pl.multiple_of(c * HALF_COLS, 128), HALF_COLS)
    return [(ref.at[pl.ds(start, count), :], dst.at[pl.ds(row, count), cols])]


def front_bundle(shard):
    y, c, _, _ = places()
    mine = lax.dynamic_slice(shard, (y * 48, c * HALF_COLS), (48, HALF_COLS))
    both = lax.dynamic_slice(shard, (0, c * HALF_COLS), (96, HALF_COLS))
    return Fetch([shard], mine, both, 80)


def fetch_rest(up_shard, down_shard):
    d = lax.axis_index("dp")
    up_part = lax.dynamic_slice(up_shard, (0, d * D), (96, D))
    down_part = lax.dynamic_slice_in_dim(down_shard, d * 96, 96, 0)
    gathered = lax.all_gather(jnp.concatenate([up_part, down_part], axis=0), ("fsdp", "dp"), axis=0)
    gathered = gathered.reshape(8, 4, 192, D)

    def up_plan(refs, dst):
        dst = dst.reshape(8, 96, FF)
        return [(refs[0].at[:, d, 0:96, :], dst.at[:, :, D * d : D * d + D]) for d in range(4)]

    def down_plan(refs, dst):
        dst = dst.reshape(8, 4, 96, D)
        return [(refs[0].at[2 * d : 2 * d + 2, :, 96:192, :], dst.at[2 * d : 2 * d + 2]) for d in range(4)]

    return [far(gathered)], (up_plan, down_plan), 4


def share_rows(rows, works):
    parts, done = [rows], None
    for work, shifts in zip(works, ([dict(dz=r) for r in (1, 2, 3)], [dict(dx=1)], [dict(dy=1), dict(dc=1)])):
        rows = jnp.concatenate(parts, axis=0) if len(parts) > 1 else rows
        if done is not None:
            rows, done = lax.optimization_barrier((rows, done))
        parts = [rows] + [exchange(rows, **shift) for shift in shifts]
        done = work(done)
    near, across, core = parts
    across, done = lax.optimization_barrier((across, done))
    return [near, across, core, exchange(across, dc=1)], done


def body(
    tuned, dp, tokens, task_ids, logit_grads, prompts, head_weights, qkv_weight, out_weight, up_weight, down_weight,
    attn_gain, mlp_gain, final_gain,
):
    rows_n = tokens.shape[0] * tokens.shape[1]
    images = rows_n * IMGS_ROW
    front_shard = jnp.concatenate([qkv_weight, out_weight], axis=1)
    gains = [gain.reshape(1, D) for gain in (attn_gain, mlp_gain, final_gain)]
    ids = task_ids.reshape(rows_n, IMGS_ROW)
    prompt_rows = prompts.transpose(1, 0, 2).reshape(PROMPTS * TASKS, D)
    resid, normed = assemble(ids, tokens.reshape(rows_n, ROW, D), prompt_rows, gains[0])
    token_rows = tokens.reshape(rows_n, ROW, D)
    ids_col = ids.reshape(images, 1)
    head_rows = head_weights.transpose(2, 0, 1).reshape(CLASSES * TASKS, D)
    grads = jnp.concatenate(
        [logit_grads.reshape(images, CLASSES), jnp.broadcast_to(ids_col, (images, 128 - CLASSES)).astype(BF16)], axis=1
    )
    tie = lambda *values: lax.optimization_barrier(values)
    if tuned:
        feed_weights = fetch_rest(up_weight, down_weight)
        front_in = front_bundle(front_shard)
        front_in.along_z()
        front_in.beside()
        resid, normed = assemble(ids, token_rows, prompt_rows, gains[0])
        front_in.column, normed = tie(front_in.column, normed)
        front_in.across()
        front_in.diagonal()
        plan_front = lambda refs, dst: own_rows(refs[0], dst) + front_in.plan(refs[1:], dst, put_front)
        fetched = [far(piece) for piece in front_in.pieces()], plan_front, 1 + 2 * (2 + 9 + 4)
    else:
        feed_weights = [gather_rows(w, dp) for w in (up_weight, down_weight)], (copy_whole(0), copy_whole(1)), 1
        resid, normed = assemble(ids, token_rows, prompt_rows, gains[0])
        fetched = [gather_rows(front_shard, dp)], copy_whole(0), 1
    *attended, middle, normed_two, front = attend(normed, resid, gains[1], *fetched)
    sent, weights, routes, d_class, d_middle, up_all, down_all = class_path(
        loss_grads(ids_col, grads, head_rows), grads, gains, [*attended, front], feed_weights
    )

    def feed_rows(rows, chain):
        for row in rows:
            chain = feed(normed_two, middle, up_all, down_all, row, rows_n, chain)
        return chain

    works = (
        lambda done: (token_grads(resid, weights, routes, d_class, d_middle, gains[0]), None),
        lambda done: (done[0], feed_rows(range(rows_n // 2), None)),
        lambda done: (done[0], feed_rows(range(rows_n // 2, rows_n), done[1])),
    )
    if tuned:
        parts, (input_grads, activations) = share_rows(sent, works)
    else:
        parts = [lax.all_gather(sent, ("dp", "fsdp"), axis=0, tiled=True)]
        input_grads, activations = works[2](works[1](works[0](None)))
    prompt_out, head_out = sums(front, prompt_rows, gains[0], parts)
    return (
        activations.reshape(tokens.shape),
        input_grads.reshape(tokens.shape),
        prompt_out.reshape(PROMPTS, TASKS, D).transpose(1, 0, 2),
        head_out.reshape(CLASSES, TASKS, D).transpose(1, 2, 0),
    )


def solution(mesh):
    rows = P(None, ("dp", "fsdp"), None, None)
    in_specs = (rows, P(None, ("dp", "fsdp"), None), rows, P(), P(), *(P("fsdp", None),) * 4, P(), P(), P())
    return jax.shard_map(
        functools.partial(body, dict(mesh.shape) == {"dp": 4, "fsdp": 8}, mesh.shape["dp"]),
        mesh=mesh,
        in_specs=in_specs,
        out_specs=(rows, rows, P(), P()),
        check_vma=False,
    )
```

```python
import functools

import jax
import jax.numpy as jnp
import numpy as np
from jax import lax
from jax.experimental import pallas as pl
from jax.experimental.pallas import tpu as pltpu
from jax.sharding import PartitionSpec as P

D = 768
HEADS = 12
HDIM = 64
FF = 3072
CLASSES = 100
TASKS = 8
PROMPTS = 50
IMG = 247
IMGS_ROW = 4
ROW = 1024
MB = 2

BLOCK = 256
TAIL = BLOCK - IMG
TAIL_AT = IMGS_ROW * IMG
SPARE = 8
HEADS_PAD = 16
SLOTS = 64
EPSILON = 1e-06
MASKED_SCORE = -1e30
BF16 = jnp.bfloat16
F32 = jnp.float32


def dot(lhs, rhs):
    return lax.dot_general(lhs, rhs, (((1,), (0,)), ((), ())), preferred_element_type=F32)


def dot_t(lhs, rhs):
    return lax.dot_general(lhs, rhs, (((1,), (1,)), ((), ())), preferred_element_type=F32)


def unit_norm(rows):
    centred = rows - jnp.mean(rows, axis=-1, keepdims=True)
    inv_std = lax.rsqrt(jnp.mean(centred * centred, axis=-1, keepdims=True) + EPSILON)
    return centred * inv_std, inv_std


def norm_back(grad_out, unit_rows, inv_std, gain):
    scaled = grad_out * gain
    inner_mean = jnp.mean(scaled * unit_rows, axis=-1, keepdims=True)
    return inv_std * (scaled - jnp.mean(scaled, axis=-1, keepdims=True) - unit_rows * inner_mean)


def gelu(rows):
    return 0.5 * rows * (1.0 + lax.erf(rows * np.float32(np.sqrt(0.5))))


def gelu_slope(rows):
    upper = 0.5 * (1.0 + lax.erf(rows * np.float32(np.sqrt(0.5))))
    return upper + rows * jnp.exp(-0.5 * rows * rows) * np.float32(1.0 / np.sqrt(2.0 * np.pi))


def params(mib):
    return pltpu.CompilerParams(vmem_limit_bytes=mib << 20)


def cost(gflops, mbytes):
    return pl.CostEstimate(flops=int(gflops * 1e9), bytes_accessed=int(mbytes * 1e6), transcendentals=0)


def far(array):
    return pltpu.with_memory_space_constraint(array, pltpu.HBM)


def whole(array):
    return pl.BlockSpec(array.shape, lambda *grid: (0,) * array.ndim, pipeline_mode=pl.Buffered(1))


def make_copies(pairs, sems, first=0):
    return [pltpu.make_async_copy(src, dst, sems.at[first + k]) for k, (src, dst) in enumerate(pairs)]


def start_copies(pairs, sems):
    copies = make_copies(pairs, sems)
    for copy in copies:
        copy.start()
    return copies


def run_copies(pairs, sems):
    for copy in start_copies(pairs, sems):
        copy.wait()


LANES = 128
STRIDED_ROWS = -(-PROMPTS // 8) * 8 * TASKS
LANE_BLOCKS = [slice(at, at + LANES) for at in range(0, D, LANES)]


def by_lanes(buf, rows):
    for block, lanes in enumerate(LANE_BLOCKS):
        buf[block, : rows.shape[0]] = rows[:, lanes]


def read_strided(buf, start, count):
    at = pl.ds(start, count, stride=TASKS)
    return jnp.concatenate([buf[block, at] for block in range(len(LANE_BLOCKS))], axis=1)


def write_strided(buf, start, rows):
    at = pl.ds(start, rows.shape[0], stride=TASKS)
    for block, lanes in enumerate(LANE_BLOCKS):
        buf[block, at] = rows[:, lanes]


def assemble_kernel(
    ids_ref, tokens_ref, prompts_ref, gain_ref, resid_ref, normed_ref, row_buf, img_buf, prompt_buf
):
    row_at = pl.program_id(0)
    by_lanes(prompt_buf, prompts_ref[...].astype(F32))
    row_buf[:ROW] = tokens_ref[0].astype(F32)
    for img in range(IMGS_ROW):
        img_buf[0 : IMG + 1] = row_buf[img * IMG : img * IMG + IMG + 1]
        img_buf[IMG:BLOCK] = row_buf[TAIL_AT + img * TAIL : TAIL_AT + (img + 1) * TAIL]
        img_buf[1 : 1 + PROMPTS] = read_strided(prompt_buf, ids_ref[row_at, img], PROMPTS)
        rows = img_buf[:BLOCK]
        at = slice(img * BLOCK, (img + 1) * BLOCK)
        resid_ref[0, at] = rows.astype(BF16)
        unit_rows, _ = unit_norm(rows)
        normed_ref[0, at] = (unit_rows * gain_ref[...]).astype(BF16)


def assemble(ids, tokens, prompts, gain):
    rows_n = tokens.shape[0]
    row_spec = pl.BlockSpec((1, ROW, D), lambda r: (r, 0, 0))
    return pl.pallas_call(
        assemble_kernel,
        grid=(rows_n,),
        in_specs=[pl.BlockSpec(memory_space=pltpu.SMEM), row_spec, whole(prompts), whole(gain)],
        out_specs=[row_spec, row_spec],
        out_shape=[pltpu.HBM(tokens.shape, BF16)] * 2,
        scratch_shapes=[
            pltpu.VMEM((ROW + SPARE, D), F32),
            pltpu.VMEM((BLOCK + SPARE, D), F32),
            pltpu.VMEM((len(LANE_BLOCKS), STRIDED_ROWS, LANES), F32),
        ],
        compiler_params=params(20),
        cost_estimate=cost(0.1, 10),
        name="assemble",
    )(ids, tokens, prompts, gain)


def softmax_pair(queries, keys, values_ext, bias, first_half):
    halves = []
    for scale_row in first_half:
        scores = dot_t(queries * scale_row, keys) + bias
        weights = jnp.exp(scores - jnp.max(scores, axis=-1, keepdims=True)).astype(BF16)
        summed = dot(weights, values_ext)
        halves.append(summed[:, :128] / summed[:, 128:])
    lanes = lax.broadcasted_iota(jnp.int32, halves[0].shape, 1)
    return jnp.where(lanes < HDIM, halves[0], halves[1])


def attend_kernel(plan, normed_ref, resid_ref, gain_ref, *refs):
    pieces, refs = refs[:-12], refs[-12:]
    query_ref, probs_ref, class_ref, kv_ref, middle_ref, normed_two_ref, front_out = refs[:7]
    packed_buf, tail_buf, tail_context, front_ref, sems = refs[7:]
    img = pl.program_id(1)
    at = pl.program_id(0) * IMGS_ROW + img
    lane = lax.broadcasted_iota(jnp.int32, (1, 128), 1)
    scale = HDIM ** (-0.5)
    halves = [
        jnp.where(lane < HDIM, scale, 0.0).astype(BF16),
        jnp.where(lane < HDIM, 0.0, scale).astype(BF16),
    ]

    kept = pltpu.make_async_copy(front_ref, front_out, sems.at[0])

    @pl.when(at == 0)
    def _():
        run_copies(plan(pieces, front_ref), sems)
        kept.start()

    @pl.when(at == pl.num_programs(0) * IMGS_ROW - 1)
    def _():
        kept.wait()

    @pl.when(img == 0)
    def _():
        ends = [normed_ref[0, end - 16 : end, :] for end in range(BLOCK, ROW + 1, BLOCK)]
        tail_buf[...] = dot(jnp.concatenate(ends, axis=0), front_ref[:, : 3 * D]).astype(BF16)
        tail_at = lax.broadcasted_iota(jnp.int32, (1, 16 * IMGS_ROW), 1)
        tail_bias = jnp.where(tail_at % 16 >= 16 - TAIL, 0.0, MASKED_SCORE)
        tail_ones = jnp.ones((16 * IMGS_ROW, 128), BF16)
        for pair in range(HEADS // 2):
            q, k, v = (tail_buf[:, part * D + pair * 128 : part * D + (pair + 1) * 128] for part in range(3))
            tail_context[:, pair * 128 : (pair + 1) * 128] = softmax_pair(
                q, k, jnp.concatenate([v, tail_ones], axis=1), tail_bias, halves
            )

    tokens = normed_ref[0, pl.ds(pl.multiple_of(img * BLOCK, BLOCK), BLOCK), :]
    for part in range(3):
        cols = slice(part * D, (part + 1) * D)
        packed_buf[:, cols] = dot(tokens, front_ref[:, cols]).astype(BF16)
    kv_ref[0] = packed_buf[:, D:]
    query_ref[at] = packed_buf[:16, :D]
    key_at = lax.broadcasted_iota(jnp.int32, (1, BLOCK), 1)
    bias = jnp.where(key_at < IMG, 0.0, MASKED_SCORE)
    queries = packed_buf[0:1, :D] * head_rows_mask().astype(BF16) * np.float32(scale).astype(BF16)
    scores = dot_t(queries, packed_buf[:, D : 2 * D]) + bias
    probs = jnp.exp(scores - jnp.max(scores, axis=-1, keepdims=True))
    probs_ref[at] = probs / jnp.sum(probs, axis=-1, keepdims=True)
    ones = jnp.ones((BLOCK, 128), BF16)
    is_tail = lax.broadcasted_iota(jnp.int32, (16, D), 0) >= 16 - TAIL
    context = []
    for pair in range(HEADS // 2):
        q, k, v = (packed_buf[:, part * D + pair * 128 : part * D + (pair + 1) * 128] for part in range(3))
        context.append(softmax_pair(q, k, jnp.concatenate([v, ones], axis=1), bias, halves))
    context = jnp.concatenate(context, axis=1)
    tail = tail_context[pl.ds(pl.multiple_of(img * 16, 16), 16), :]
    last = jnp.where(is_tail, tail, context[BLOCK - 16 :])
    context = jnp.concatenate([context[: BLOCK - 16], last], axis=0).astype(BF16)
    middle = resid_ref[0].astype(F32) + dot(context, front_ref[:, 3 * D :])
    middle_ref[...] = middle
    class_ref[at] = middle[:8]
    normed_two_ref[...] = (unit_norm(middle)[0] * gain_ref[...]).astype(BF16)


def head_rows_mask():
    return (
        lax.broadcasted_iota(jnp.int32, (HEADS_PAD, D), 1) // HDIM
        == lax.broadcasted_iota(jnp.int32, (HEADS_PAD, D), 0)
    ).astype(F32)


def attend(normed, resid, gain, pieces, plan, copies_n):
    rows_n = normed.shape[0]
    images = rows_n * IMGS_ROW
    near = pl.BlockSpec(memory_space=pltpu.VMEM)
    flat = pl.BlockSpec((BLOCK, D), lambda r, i: (r * IMGS_ROW + i, 0))
    return pl.pallas_call(
        functools.partial(attend_kernel, plan),
        grid=(rows_n, IMGS_ROW),
        in_specs=[
            pl.BlockSpec((1, ROW, D), lambda r, i: (r, 0, 0)),
            pl.BlockSpec((1, BLOCK, D), lambda r, i: (r, i, 0)),
            whole(gain),
        ]
        + [pl.BlockSpec(memory_space=pltpu.HBM)] * len(pieces),
        out_specs=[near] * 3
        + [
            pl.BlockSpec((1, BLOCK, 2 * D), lambda r, i: (r * IMGS_ROW + i, 0, 0)),
            flat,
            flat,
            pl.BlockSpec(memory_space=pltpu.HBM),
        ],
        out_shape=[
            pltpu.VMEM((images, 16, D), BF16),
            pltpu.VMEM((images, HEADS_PAD, BLOCK), F32),
            pltpu.VMEM((images, 8, D), F32),
            pltpu.HBM((images, BLOCK, 2 * D), BF16),
            pltpu.HBM((rows_n * ROW, D), F32),
            pltpu.HBM((rows_n * ROW, D), BF16),
            pltpu.HBM((D, 4 * D), BF16),
        ],
        scratch_shapes=[
            pltpu.VMEM((BLOCK, 3 * D), BF16),
            pltpu.VMEM((16 * IMGS_ROW, 3 * D), BF16),
            pltpu.VMEM((16 * IMGS_ROW, D), F32),
            pltpu.VMEM((D, 4 * D), BF16),
            pltpu.SemaphoreType.DMA((copies_n,)),
        ],
        compiler_params=params(24),
        cost_estimate=cost(8 * rows_n, 15 * rows_n),
        name="attend",
    )(far(normed), far(resid), gain, *pieces)


def loss_kernel(ids_ref, grads_ref, heads_ref, d_final_ref):
    images = ids_ref.shape[0]
    spread = (
        lax.broadcasted_iota(jnp.int32, (128, CLASSES * TASKS), 1) // TASKS
        == lax.broadcasted_iota(jnp.int32, (128, CLASSES * TASKS), 0)
    ).astype(F32).astype(BF16)
    task_at = lax.broadcasted_iota(jnp.int32, (images, CLASSES * TASKS), 1) % TASKS
    chosen = jnp.where(ids_ref[...] == task_at, dot(grads_ref[...], spread), 0.0).astype(BF16)
    d_final_ref[...] = dot(chosen, heads_ref[...])


def loss_grads(ids, grads, heads):
    operands = (ids, grads, heads)
    out = jax.ShapeDtypeStruct((ids.shape[0], D), F32)
    return pl.pallas_call(
        loss_kernel,
        grid=(1,),
        in_specs=[whole(o) for o in operands],
        out_specs=whole(out),
        out_shape=out,
        compiler_params=params(12),
        cost_estimate=cost(0.1, 2),
        name="loss_grads",
    )(*operands)


def class_kernel(
    plans, d_final_ref, grads_ref, mlp_gain_ref, final_gain_ref,
    queries_ref, probs_ref, middles_ref, kv_hbm, front_hbm, *refs,
):
    feed_refs = refs[:-14]
    (
        sent_ref, weights_ref, routes_ref, d_class_ref, d_middle_ref, up_ref, down_ref,
        score_slots, prob_slots, kv_ref, front_ref, sems, up_sems, down_sems,
    ) = refs[-14:]
    images = middles_ref.shape[0]
    up_copies = make_copies(plans[0](feed_refs, up_ref), up_sems)
    down_copies = make_copies(plans[1](feed_refs, down_ref), down_sems)
    for pair in zip(up_copies, down_copies):
        for copy in pair:
            copy.start()
    front_copy, kv_copy = start_copies([(front_hbm, front_ref), (kv_hbm, kv_ref)], sems)
    mlp_gain, final_gain = mlp_gain_ref[...], final_gain_ref[...]
    middle = middles_ref[:, 0, :]
    unit_mlp, inv_mlp = unit_norm(middle)
    normed = (unit_mlp * mlp_gain).astype(BF16)
    output, pre = middle, []
    width = FF // len(up_copies)
    for at, (up_copy, down_copy) in enumerate(zip(up_copies, down_copies)):
        cols = slice(at * width, (at + 1) * width)
        up_copy.wait()
        pre.append(dot(normed, up_ref[:, cols]))
        down_copy.wait()
        output = output + dot(gelu(pre[-1]).astype(BF16), down_ref[cols, :])
    pre = jnp.concatenate(pre, axis=1)
    unit_fin, inv_fin = unit_norm(output)
    sent_ref[:, 2 * D : 3 * D] = (unit_fin * final_gain).astype(BF16)
    d_output = norm_back(d_final_ref[...], unit_fin, inv_fin, final_gain)
    d_act = dot_t(d_output.astype(BF16), down_ref[...])
    d_pre = (d_act * gelu_slope(pre)).astype(BF16)
    d_middle = d_output + norm_back(dot_t(d_pre, up_ref[...]), unit_mlp, inv_mlp, mlp_gain)
    d_middle_ref[:images] = d_middle
    front_copy.wait()
    d_context = dot_t(d_middle.astype(BF16), front_ref[:, 3 * D :]).astype(BF16)
    sent_ref[:, 3 * D : 4 * D] = d_context
    of_head = head_rows_mask()
    scale = HDIM ** (-0.5)
    kv_copy.wait()
    queries = jnp.concatenate([queries_ref[img, 0:1, :] for img in range(images)], axis=0)
    sent_ref[:, :D] = queries
    spread_heads = lambda rows: (rows[:, None, :] * of_head[None]).reshape(images * HEADS_PAD, D).astype(BF16)
    by_head = spread_heads(d_context.astype(F32))
    probs = probs_ref[...].reshape(images * HEADS_PAD, BLOCK)
    rows_of = lambda array, img: array[img * HEADS_PAD : (img + 1) * HEADS_PAD]
    d_probs = jnp.concatenate(
        [dot_t(rows_of(by_head, img), kv_ref[img, :, D:]) for img in range(images)], axis=0
    )
    d_scores = probs * (d_probs - jnp.sum(probs * d_probs, axis=-1, keepdims=True))
    score_slots[...] = d_scores[:, :128]
    prob_slots[...] = probs[:, :128]
    d_scores = d_scores.astype(BF16)
    weights_ref[:, :HEADS_PAD] = d_scores.reshape(images, HEADS_PAD, BLOCK)
    weights_ref[:, HEADS_PAD:] = probs.astype(BF16).reshape(images, HEADS_PAD, BLOCK)
    d_queries = jnp.concatenate(
        [
            jnp.sum(dot(rows_of(d_scores, img), kv_ref[img, :, :D]) * of_head, axis=0, keepdims=True)
            for img in range(images)
        ],
        axis=0,
    )
    lane = lax.broadcasted_iota(jnp.int32, (images, 128), 1)
    for slots, start in ((prob_slots, D), (score_slots, 4 * D)):
        for pair in range(HEADS // 2):
            first, second = (slots[pl.ds(2 * pair + h, images, stride=HEADS_PAD)] for h in range(2))
            both = jnp.where(lane < SLOTS, first, pltpu.roll(second, SLOTS, 1))
            sent_ref[:, start + pair * 128 : start + (pair + 1) * 128] = both.astype(BF16)
    sent_ref[:, 5 * D :] = grads_ref[...]
    by_key = dot_t(spread_heads(queries.astype(F32) * scale), front_ref[:, D : 2 * D]).astype(BF16)
    by_value = dot_t(by_head, front_ref[:, 2 * D : 3 * D]).astype(BF16)
    routes_ref[:, :HEADS_PAD] = by_key.reshape(images, HEADS_PAD, D)
    routes_ref[:, HEADS_PAD:] = by_value.reshape(images, HEADS_PAD, D)
    d_class_ref[:images] = dot_t((d_queries * scale).astype(BF16), front_ref[:, :D])


SENT = 5 * D + 128


def class_path(d_final, grads, gains, attended, feed_weights):
    images = d_final.shape[0]
    *small, kv, front = attended
    operands = (d_final, grads, *gains[1:], *small)
    feed_arrays, plans, copies_n = feed_weights
    remote = (far(kv), far(front), *feed_arrays)
    outs = [
        jax.ShapeDtypeStruct((images, SENT), BF16),
        jax.ShapeDtypeStruct((images, 2 * HEADS_PAD, BLOCK), BF16),
        jax.ShapeDtypeStruct((images, 2 * HEADS_PAD, D), BF16),
        jax.ShapeDtypeStruct((images + SPARE, D), F32),
        jax.ShapeDtypeStruct((images + SPARE, D), F32),
        pltpu.VMEM((D, FF), BF16),
        pltpu.VMEM((FF, D), BF16),
    ]
    near = pl.BlockSpec(memory_space=pltpu.VMEM)
    return pl.pallas_call(
        functools.partial(class_kernel, plans),
        in_specs=[near] * len(operands) + [pl.BlockSpec(memory_space=pltpu.HBM)] * len(remote),
        out_specs=[near] * len(outs),
        out_shape=outs,
        scratch_shapes=[
            pltpu.VMEM((images * HEADS_PAD, 128), F32),
            pltpu.VMEM((images * HEADS_PAD, 128), F32),
            pltpu.VMEM(kv.shape, BF16),
            pltpu.VMEM((D, 4 * D), BF16),
            pltpu.SemaphoreType.DMA((2,)),
            pltpu.SemaphoreType.DMA((copies_n,)),
            pltpu.SemaphoreType.DMA((copies_n,)),
        ],
        compiler_params=params(24),
        cost_estimate=cost(8, 30),
        name="class_path",
    )(*operands, *remote)


FF_STEP = 768


def feed_kernel(normed_ref, middle_ref, up_ref, down_ref, *refs):
    out_ref, row_buf = refs[-2:]
    img = pl.program_id(0)
    rows = normed_ref[...]
    total = middle_ref[...]
    for step in range(FF // FF_STEP):
        at = slice(step * FF_STEP, (step + 1) * FF_STEP)
        total = total + dot(gelu(dot(rows, up_ref[:, at])).astype(BF16), down_ref[at, :])
    for at in range(IMGS_ROW):

        @pl.when(img == at)
        def _():
            row_buf[at * IMG : (at + 1) * IMG] = total[:IMG]
            row_buf[TAIL_AT + at * TAIL : TAIL_AT + (at + 1) * TAIL] = total[IMG:]

    @pl.when(img == IMGS_ROW - 1)
    def _():
        out_ref[0] = row_buf[:ROW].astype(BF16)


def feed(normed, middle, up_all, down_all, row, rows_n, chain):
    spec = pl.BlockSpec((BLOCK, D), lambda i: (row * IMGS_ROW + i, 0))
    chained = [] if chain is None else [chain]
    return pl.pallas_call(
        feed_kernel,
        grid=(IMGS_ROW,),
        in_specs=[spec, spec]
        + [pl.BlockSpec(memory_space=pltpu.VMEM)] * 2
        + [pl.BlockSpec(memory_space=pltpu.HBM)] * len(chained),
        out_specs=pl.BlockSpec((1, ROW, D), lambda i: (row, 0, 0)),
        out_shape=pltpu.HBM((rows_n, ROW, D), BF16),
        input_output_aliases={} if chain is None else {4: 0},
        scratch_shapes=[pltpu.VMEM((ROW + SPARE, D), F32)],
        compiler_params=params(18),
        cost_estimate=cost(10, 20),
        name="feed",
    )(far(normed), far(middle), up_all, down_all, *chained)


def token_grads_kernel(resid_ref, weights_ref, routes_ref, d_class_ref, d_middle_ref, gain_ref, out_ref):
    row_at = pl.program_id(0)
    gain = gain_ref[...]
    place = lax.broadcasted_iota(jnp.int32, (BLOCK, 1), 0)
    is_class = (place == 0).astype(F32)
    keep = jnp.where((place == 0) | (place > PROMPTS), 1.0, 0.0)
    zeros_at = TAIL_AT // 8 * 8
    out_ref[0, zeros_at:] = jnp.zeros((ROW - zeros_at, D), F32)
    for img in range(IMGS_ROW):
        one = pl.ds(row_at * IMGS_ROW + img, 1)
        unit_rows, inv_std = unit_norm(resid_ref[0, img * BLOCK : (img + 1) * BLOCK].astype(F32))
        d_normed = lax.dot_general(
            weights_ref[img], routes_ref[img], (((0,), (0,)), ((), ())), preferred_element_type=F32
        )
        d_normed = d_normed + is_class * d_class_ref[one]
        d_resid = norm_back(d_normed, unit_rows, inv_std, gain) + is_class * d_middle_ref[one]
        out_ref[0, img * IMG : (img + 1) * IMG] = (d_resid * keep)[:IMG]


def token_grads(resid, weights, routes, d_class, d_middle, gain):
    rows_n = resid.shape[0]
    row_spec = pl.BlockSpec((1, ROW, D), lambda r: (r, 0, 0))
    img_spec = lambda width: pl.BlockSpec((IMGS_ROW, 2 * HEADS_PAD, width), lambda r: (r, 0, 0))
    return pl.pallas_call(
        token_grads_kernel,
        grid=(rows_n,),
        in_specs=[row_spec, img_spec(BLOCK), img_spec(D), whole(d_class), whole(d_middle), whole(gain)],
        out_specs=row_spec,
        out_shape=pltpu.HBM(resid.shape, F32),
        compiler_params=params(20),
        cost_estimate=cost(0.5, 20),
        name="token_grads",
    )(far(resid), weights, routes, d_class, d_middle, gain)


def sums_kernel(front_ref, prompts_ref, gain_ref, *refs):
    parts, (prompt_out, head_out, all_buf, sum_buf, prompt_buf, sems) = refs[:-6], refs[-6:]
    rows = parts[0].shape[0]
    run_copies([(part, all_buf.at[pl.ds(at * rows, rows), :]) for at, part in enumerate(parts)], sems)
    scale = np.float32(HDIM ** (-0.5)).astype(BF16)
    column = lambda at: all_buf[:, at * D : (at + 1) * D]
    by_class = all_buf[:, 5 * D :].T
    ids = by_class[CLASSES : CLASSES + 1].astype(F32)
    masks = [(ids == task).astype(F32).astype(BF16) for task in range(TASKS)]
    of_task = (lax.broadcasted_iota(jnp.int32, (TASKS, 1), 0).astype(F32) == ids).astype(F32)
    spread = by_class[:CLASSES].astype(F32)[:, None, :] * of_task[None]
    head_out[...] = dot(spread.reshape(CLASSES * TASKS, -1).astype(BF16), column(2))
    lane = lax.broadcasted_iota(jnp.int32, (SLOTS, 128), 1)
    for side, (slots, lane_rows) in enumerate(((column(4), column(0) * scale), (column(1), column(3)))):
        slots = slots.T
        for pair in range(HEADS // 2):
            at = slice(pair * 128, (pair + 1) * 128)
            summed = dot(jnp.concatenate([slots[at] * mask for mask in masks], axis=0), lane_rows[:, at])
            for task in range(TASKS):
                first, second = (summed[task * 128 + h * SLOTS : task * 128 + (h + 1) * SLOTS] for h in range(2))
                sum_buf[task * SLOTS : (task + 1) * SLOTS, side * D + pair * 128 : side * D + (pair + 1) * 128] = (
                    jnp.where(lane < HDIM, first, second).astype(BF16)
                )
    d_normed = dot_t(sum_buf[...], front_ref[:, D : 3 * D])
    by_lanes(prompt_buf, prompts_ref[...].astype(F32))
    for task in range(TASKS):
        unit_rows, inv_std = unit_norm(read_strided(prompt_buf, task, PROMPTS))
        d_task = d_normed[task * SLOTS + 1 : task * SLOTS + 1 + PROMPTS]
        write_strided(prompt_buf, task, norm_back(d_task, unit_rows, inv_std, gain_ref[...]))
    for block, lanes in enumerate(LANE_BLOCKS):
        prompt_out[:, lanes] = prompt_buf[block, : PROMPTS * TASKS]


def sums(front, prompts, gain, parts):
    operands = (front, prompts, gain)
    outs = [
        jax.ShapeDtypeStruct((PROMPTS * TASKS, D), F32),
        jax.ShapeDtypeStruct((CLASSES * TASKS, D), F32),
    ]
    images = sum(part.shape[0] for part in parts)
    return pl.pallas_call(
        sums_kernel,
        grid=(1,),
        in_specs=[pl.BlockSpec(memory_space=pltpu.VMEM)] * len(operands)
        + [pl.BlockSpec(memory_space=pl.ANY)] * len(parts),
        out_specs=[whole(o) for o in outs],
        out_shape=outs,
        scratch_shapes=[
            pltpu.VMEM((images, SENT), BF16),
            pltpu.VMEM((TASKS * SLOTS, 2 * D), BF16),
            pltpu.VMEM((len(LANE_BLOCKS), STRIDED_ROWS, LANES), F32),
            pltpu.SemaphoreType.DMA((len(parts),)),
        ],
        compiler_params=params(28 if images <= 512 else 60),
        cost_estimate=cost(5, 15),
        name="sums",
    )(*operands, *parts)


def gather_rows(shard, dp):
    part = shard.shape[0] // dp
    mine = lax.dynamic_slice_in_dim(shard, lax.axis_index("dp") * part, part, 0)
    return lax.all_gather(mine, ("fsdp", "dp"), axis=0, tiled=True)


def copy_whole(at):
    return lambda refs, dst: [(refs[at], dst)]


def places():
    d, f = lax.axis_index("dp"), lax.axis_index("fsdp")
    return d // 2, d % 2, f // 2, f % 2


def exchange(value, dy=0, dc=0, dz=0, dx=0):
    pairs = []
    for at in range(32):
        y, c, z, x = at // 16, at // 8 % 2, at // 2 % 4, at % 2
        pairs.append((at, (((y ^ dy) * 2 + (c ^ dc)) * 4 + (z ^ dz)) * 2 + (x ^ dx)))
    return lax.ppermute(value, ("dp", "fsdp"), pairs)


HALF_COLS = 2 * D


class Fetch:
    def __init__(self, own, mine, both, cut):
        self.own, self.mine, self.both, self.cut, self.half = own, mine, both, cut, mine.shape[0]

    def along_z(self):
        self.column = jnp.concatenate([exchange(self.mine, dz=r) for r in (1, 2, 3)], axis=0)

    def beside(self):
        self.own_x = exchange(self.both, dx=1)

    def across(self):
        self.over_x = exchange(self.column, dx=1)
        self.over_y = exchange(self.column, dy=1)

    def diagonal(self):
        self.diag_y = exchange(self.over_x[: self.cut], dy=1)
        self.diag_x = exchange(self.over_y[self.cut :], dx=1)

    def pieces(self):
        near = [self.own_x, self.column, self.over_x, self.over_y, self.diag_y, self.diag_x]
        return self.own + near + [exchange(piece, dc=1) for piece in near]

    def plan(self, refs, dst, put):
        y, c, z, x = places()
        half, cut = self.half, self.cut
        pairs = []
        for side in range(2):
            own_x, column, over_x, over_y, diag_y, diag_x = refs[6 * side : 6 + 6 * side]

            def add(ref, start, count, r, x_at, y_at, within=0):
                return put(ref, start, count, dst, (z ^ r) * 2 + x_at, y_at, c ^ side, within)

            for y_at in range(2):
                pairs += add(own_x, y_at * half, half, 0, x ^ 1, y_at)
            for r in (1, 2, 3):
                start = (r - 1) * half
                pairs += add(column, start, half, r, x, y)
                pairs += add(over_x, start, half, r, x ^ 1, y)
                pairs += add(over_y, start, half, r, x, y ^ 1)
                first = min(max(cut - start, 0), half)
                if first:
                    pairs += add(diag_y, start, first, r, x ^ 1, y ^ 1)
                if first < half:
                    pairs += add(diag_x, start + first - cut, half - first, r, x ^ 1, y ^ 1, first)
        return pairs


def own_rows(ref, dst):
    _, _, z, x = places()
    count = ref.shape[0]
    return [(ref, dst.at[pl.ds(pl.multiple_of((z * 2 + x) * count, count), count), :])]


def put_front(ref, start, count, dst, place, y, c, within):
    row = pl.multiple_of(place * 96 + y * 48 + within, 16)
    cols = pl.ds(pl.multiple_of(c * HALF_COLS, 128), HALF_COLS)
    return [(ref.at[pl.ds(start, count), :], dst.at[pl.ds(row, count), cols])]


def front_bundle(shard):
    y, c, _, _ = places()
    mine = lax.dynamic_slice(shard, (y * 48, c * HALF_COLS), (48, HALF_COLS))
    both = lax.dynamic_slice(shard, (0, c * HALF_COLS), (96, HALF_COLS))
    return Fetch([shard], mine, both, 80)


def fetch_rest(up_shard, down_shard):
    d = lax.axis_index("dp")
    up_part = lax.dynamic_slice(up_shard, (0, d * D), (96, D))
    down_part = lax.dynamic_slice_in_dim(down_shard, d * 96, 96, 0)
    gathered = lax.all_gather(jnp.concatenate([up_part, down_part], axis=0), ("fsdp", "dp"), axis=0)
    gathered = gathered.reshape(8, 4, 192, D)

    def up_plan(refs, dst):
        dst = dst.reshape(8, 96, FF)
        return [(refs[0].at[:, d, 0:96, :], dst.at[:, :, D * d : D * d + D]) for d in range(4)]

    def down_plan(refs, dst):
        dst = dst.reshape(8, 4, 96, D)
        return [(refs[0].at[2 * d : 2 * d + 2, :, 96:192, :], dst.at[2 * d : 2 * d + 2]) for d in range(4)]

    return [far(gathered)], (up_plan, down_plan), 4


def share_rows(rows, works):
    parts, done = [rows], None
    for work, shifts in zip(works, ([dict(dz=r) for r in (1, 2, 3)], [dict(dx=1)], [dict(dy=1), dict(dc=1)])):
        rows = jnp.concatenate(parts, axis=0) if len(parts) > 1 else rows
        if done is not None:
            rows, done = lax.optimization_barrier((rows, done))
        parts = [rows] + [exchange(rows, **shift) for shift in shifts]
        done = work(done)
    near, across, core = parts
    across, done = lax.optimization_barrier((across, done))
    return [near, across, core, exchange(across, dc=1)], done


def body(
    tuned, dp, tokens, task_ids, logit_grads, prompts, head_weights, qkv_weight, out_weight, up_weight, down_weight,
    attn_gain, mlp_gain, final_gain,
):
    rows_n = tokens.shape[0] * tokens.shape[1]
    images = rows_n * IMGS_ROW
    front_shard = jnp.concatenate([qkv_weight, out_weight], axis=1)
    gains = [gain.reshape(1, D) for gain in (attn_gain, mlp_gain, final_gain)]
    ids = task_ids.reshape(rows_n, IMGS_ROW)
    prompt_rows = prompts.transpose(1, 0, 2).reshape(PROMPTS * TASKS, D)
    token_rows = tokens.reshape(rows_n, ROW, D)
    ids_col = ids.reshape(images, 1)
    head_rows = head_weights.transpose(2, 0, 1).reshape(CLASSES * TASKS, D)
    grads = jnp.concatenate(
        [logit_grads.reshape(images, CLASSES), jnp.broadcast_to(ids_col, (images, 128 - CLASSES)).astype(BF16)], axis=1
    )
    tie = lambda *values: lax.optimization_barrier(values)
    if tuned:
        feed_weights = fetch_rest(up_weight, down_weight)
        front_in = front_bundle(front_shard)
        front_in.along_z()
        front_in.beside()
        resid, normed = assemble(ids, token_rows, prompt_rows, gains[0])
        front_in.column, normed = tie(front_in.column, normed)
        front_in.across()
        front_in.diagonal()
        plan_front = lambda refs, dst: own_rows(refs[0], dst) + front_in.plan(refs[1:], dst, put_front)
        fetched = [far(piece) for piece in front_in.pieces()], plan_front, 1 + 2 * (2 + 9 + 4)
    else:
        feed_weights = [gather_rows(w, dp) for w in (up_weight, down_weight)], (copy_whole(0), copy_whole(1)), 1
        resid, normed = assemble(ids, token_rows, prompt_rows, gains[0])
        fetched = [gather_rows(front_shard, dp)], copy_whole(0), 1
    *attended, middle, normed_two, front = attend(normed, resid, gains[1], *fetched)
    sent, weights, routes, d_class, d_middle, up_all, down_all = class_path(
        loss_grads(ids_col, grads, head_rows), grads, gains, [*attended, front], feed_weights
    )

    def feed_rows(rows, chain):
        for row in rows:
            chain = feed(normed_two, middle, up_all, down_all, row, rows_n, chain)
        return chain

    works = (
        lambda done: (token_grads(resid, weights, routes, d_class, d_middle, gains[0]), None),
        lambda done: (done[0], feed_rows(range(rows_n // 2), None)),
        lambda done: (done[0], feed_rows(range(rows_n // 2, rows_n), done[1])),
    )
    if tuned:
        parts, (input_grads, activations) = share_rows(sent, works)
    else:
        parts = [lax.all_gather(sent, ("dp", "fsdp"), axis=0, tiled=True)]
        input_grads, activations = works[2](works[1](works[0](None)))
    prompt_out, head_out = sums(front, prompt_rows, gains[0], parts)
    return (
        activations.reshape(tokens.shape),
        input_grads.reshape(tokens.shape),
        prompt_out.reshape(PROMPTS, TASKS, D).transpose(1, 0, 2),
        head_out.reshape(CLASSES, TASKS, D).transpose(1, 2, 0),
    )


def solution(mesh):
    rows = P(None, ("dp", "fsdp"), None, None)
    in_specs = (rows, P(None, ("dp", "fsdp"), None), rows, P(), P(), *(P("fsdp", None),) * 4, P(), P(), P())
    return jax.shard_map(
        functools.partial(body, dict(mesh.shape) == {"dp": 4, "fsdp": 8}, mesh.shape["dp"]),
        mesh=mesh,
        in_specs=in_specs,
        out_specs=(rows, rows, P(), P()),
        check_vma=False,
    )
```

```python
import functools

import jax
import jax.numpy as jnp
import numpy as np
from jax import lax
from jax.experimental import pallas as pl
from jax.experimental.pallas import tpu as pltpu
from jax.sharding import PartitionSpec as P

D = 768
HEADS = 12
HDIM = 64
FF = 3072
CLASSES = 100
TASKS = 8
PROMPTS = 50
IMG = 247
IMGS_ROW = 4
ROW = 1024
MB = 2

BLOCK = 256
TAIL = BLOCK - IMG
TAIL_AT = IMGS_ROW * IMG
SPARE = 8
HEADS_PAD = 16
SLOTS = 64
EPSILON = 1e-06
MASKED_SCORE = -1e30
BF16 = jnp.bfloat16
F32 = jnp.float32


def dot(lhs, rhs):
    return lax.dot_general(lhs, rhs, (((1,), (0,)), ((), ())), preferred_element_type=F32)


def dot_t(lhs, rhs):
    return lax.dot_general(lhs, rhs, (((1,), (1,)), ((), ())), preferred_element_type=F32)


def unit_norm(rows):
    centred = rows - jnp.mean(rows, axis=-1, keepdims=True)
    inv_std = lax.rsqrt(jnp.mean(centred * centred, axis=-1, keepdims=True) + EPSILON)
    return centred * inv_std, inv_std


def norm_back(grad_out, unit_rows, inv_std, gain):
    scaled = grad_out * gain
    inner_mean = jnp.mean(scaled * unit_rows, axis=-1, keepdims=True)
    return inv_std * (scaled - jnp.mean(scaled, axis=-1, keepdims=True) - unit_rows * inner_mean)


def gelu(rows):
    return 0.5 * rows * (1.0 + lax.erf(rows * np.float32(np.sqrt(0.5))))


def gelu_slope(rows):
    upper = 0.5 * (1.0 + lax.erf(rows * np.float32(np.sqrt(0.5))))
    return upper + rows * jnp.exp(-0.5 * rows * rows) * np.float32(1.0 / np.sqrt(2.0 * np.pi))


def params(mib):
    return pltpu.CompilerParams(vmem_limit_bytes=mib << 20)


def cost(gflops, mbytes):
    return pl.CostEstimate(flops=int(gflops * 1e9), bytes_accessed=int(mbytes * 1e6), transcendentals=0)


def far(array):
    return pltpu.with_memory_space_constraint(array, pltpu.HBM)


def whole(array):
    return pl.BlockSpec(array.shape, lambda *grid: (0,) * array.ndim, pipeline_mode=pl.Buffered(1))


def make_copies(pairs, sems, first=0):
    return [pltpu.make_async_copy(src, dst, sems.at[first + k]) for k, (src, dst) in enumerate(pairs)]


def start_copies(pairs, sems):
    copies = make_copies(pairs, sems)
    for copy in copies:
        copy.start()
    return copies


def run_copies(pairs, sems):
    for copy in start_copies(pairs, sems):
        copy.wait()


LANES = 128
STRIDED_ROWS = -(-PROMPTS // 8) * 8 * TASKS
LANE_BLOCKS = [slice(at, at + LANES) for at in range(0, D, LANES)]


def by_lanes(buf, rows):
    for block, lanes in enumerate(LANE_BLOCKS):
        buf[block, : rows.shape[0]] = rows[:, lanes]


def read_strided(buf, start, count):
    at = pl.ds(start, count, stride=TASKS)
    return jnp.concatenate([buf[block, at] for block in range(len(LANE_BLOCKS))], axis=1)


def write_strided(buf, start, rows):
    at = pl.ds(start, rows.shape[0], stride=TASKS)
    for block, lanes in enumerate(LANE_BLOCKS):
        buf[block, at] = rows[:, lanes]


def assemble_kernel(
    ids_ref, tokens_ref, prompts_ref, gain_ref, resid_ref, normed_ref, row_buf, img_buf, prompt_buf
):
    row_at = pl.program_id(0)
    by_lanes(prompt_buf, prompts_ref[...].astype(F32))
    row_buf[:ROW] = tokens_ref[0].astype(F32)
    for img in range(IMGS_ROW):
        img_buf[0 : IMG + 1] = row_buf[img * IMG : img * IMG + IMG + 1]
        img_buf[IMG:BLOCK] = row_buf[TAIL_AT + img * TAIL : TAIL_AT + (img + 1) * TAIL]
        img_buf[1 : 1 + PROMPTS] = read_strided(prompt_buf, ids_ref[row_at, img], PROMPTS)
        rows = img_buf[:BLOCK]
        at = slice(img * BLOCK, (img + 1) * BLOCK)
        resid_ref[0, at] = rows.astype(BF16)
        unit_rows, _ = unit_norm(rows)
        normed_ref[0, at] = (unit_rows * gain_ref[...]).astype(BF16)


def assemble(ids, tokens, prompts, gain):
    rows_n = tokens.shape[0]
    row_spec = pl.BlockSpec((1, ROW, D), lambda r: (r, 0, 0))
    return pl.pallas_call(
        assemble_kernel,
        grid=(rows_n,),
        in_specs=[pl.BlockSpec(memory_space=pltpu.SMEM), row_spec, whole(prompts), whole(gain)],
        out_specs=[row_spec, row_spec],
        out_shape=[pltpu.HBM(tokens.shape, BF16)] * 2,
        scratch_shapes=[
            pltpu.VMEM((ROW + SPARE, D), F32),
            pltpu.VMEM((BLOCK + SPARE, D), F32),
            pltpu.VMEM((len(LANE_BLOCKS), STRIDED_ROWS, LANES), F32),
        ],
        compiler_params=params(20),
        cost_estimate=cost(0.1, 10),
        name="assemble",
    )(ids, tokens, prompts, gain)


def softmax_pair(queries, keys, values_ext, bias, first_half):
    halves = []
    for scale_row in first_half:
        scores = dot_t(queries * scale_row, keys) + bias
        weights = jnp.exp(scores - jnp.max(scores, axis=-1, keepdims=True)).astype(BF16)
        summed = dot(weights, values_ext)
        halves.append(summed[:, :128] / summed[:, 128:])
    lanes = lax.broadcasted_iota(jnp.int32, halves[0].shape, 1)
    return jnp.where(lanes < HDIM, halves[0], halves[1])


def attend_kernel(plan, normed_ref, resid_ref, gain_ref, *refs):
    pieces, refs = refs[:-12], refs[-12:]
    query_ref, probs_ref, class_ref, kv_ref, middle_ref, normed_two_ref, front_out = refs[:7]
    packed_buf, tail_buf, tail_context, front_ref, sems = refs[7:]
    img = pl.program_id(1)
    at = pl.program_id(0) * IMGS_ROW + img
    lane = lax.broadcasted_iota(jnp.int32, (1, 128), 1)
    scale = HDIM ** (-0.5)
    halves = [
        jnp.where(lane < HDIM, scale, 0.0).astype(BF16),
        jnp.where(lane < HDIM, 0.0, scale).astype(BF16),
    ]

    kept = pltpu.make_async_copy(front_ref, front_out, sems.at[0])

    @pl.when(at == 0)
    def _():
        run_copies(plan(pieces, front_ref), sems)
        kept.start()

    @pl.when(at == pl.num_programs(0) * IMGS_ROW - 1)
    def _():
        kept.wait()

    @pl.when(img == 0)
    def _():
        ends = [normed_ref[0, end - 16 : end, :] for end in range(BLOCK, ROW + 1, BLOCK)]
        tail_buf[...] = dot(jnp.concatenate(ends, axis=0), front_ref[:, : 3 * D]).astype(BF16)
        tail_at = lax.broadcasted_iota(jnp.int32, (1, 16 * IMGS_ROW), 1)
        tail_bias = jnp.where(tail_at % 16 >= 16 - TAIL, 0.0, MASKED_SCORE)
        tail_ones = jnp.ones((16 * IMGS_ROW, 128), BF16)
        for pair in range(HEADS // 2):
            q, k, v = (tail_buf[:, part * D + pair * 128 : part * D + (pair + 1) * 128] for part in range(3))
            tail_context[:, pair * 128 : (pair + 1) * 128] = softmax_pair(
                q, k, jnp.concatenate([v, tail_ones], axis=1), tail_bias, halves
            )

    tokens = normed_ref[0, pl.ds(pl.multiple_of(img * BLOCK, BLOCK), BLOCK), :]
    for part in range(3):
        cols = slice(part * D, (part + 1) * D)
        packed_buf[:, cols] = dot(tokens, front_ref[:, cols]).astype(BF16)
    kv_ref[0] = packed_buf[:, D:]
    query_ref[at] = packed_buf[:16, :D]
    key_at = lax.broadcasted_iota(jnp.int32, (1, BLOCK), 1)
    bias = jnp.where(key_at < IMG, 0.0, MASKED_SCORE)
    queries = packed_buf[0:1, :D] * head_rows_mask().astype(BF16) * np.float32(scale).astype(BF16)
    scores = dot_t(queries, packed_buf[:, D : 2 * D]) + bias
    probs = jnp.exp(scores - jnp.max(scores, axis=-1, keepdims=True))
    probs_ref[at] = probs / jnp.sum(probs, axis=-1, keepdims=True)
    ones = jnp.ones((BLOCK, 128), BF16)
    is_tail = lax.broadcasted_iota(jnp.int32, (16, D), 0) >= 16 - TAIL
    context = []
    for pair in range(HEADS // 2):
        q, k, v = (packed_buf[:, part * D + pair * 128 : part * D + (pair + 1) * 128] for part in range(3))
        context.append(softmax_pair(q, k, jnp.concatenate([v, ones], axis=1), bias, halves))
    context = jnp.concatenate(context, axis=1)
    tail = tail_context[pl.ds(pl.multiple_of(img * 16, 16), 16), :]
    last = jnp.where(is_tail, tail, context[BLOCK - 16 :])
    context = jnp.concatenate([context[: BLOCK - 16], last], axis=0).astype(BF16)
    middle = resid_ref[0].astype(F32) + dot(context, front_ref[:, 3 * D :])
    middle_ref[...] = middle
    class_ref[at] = middle[:8]
    normed_two_ref[...] = (unit_norm(middle)[0] * gain_ref[...]).astype(BF16)


def head_rows_mask():
    return (
        lax.broadcasted_iota(jnp.int32, (HEADS_PAD, D), 1) // HDIM
        == lax.broadcasted_iota(jnp.int32, (HEADS_PAD, D), 0)
    ).astype(F32)


def attend(normed, resid, gain, pieces, plan, copies_n):
    rows_n = normed.shape[0]
    images = rows_n * IMGS_ROW
    near = pl.BlockSpec(memory_space=pltpu.VMEM)
    flat = pl.BlockSpec((BLOCK, D), lambda r, i: (r * IMGS_ROW + i, 0))
    return pl.pallas_call(
        functools.partial(attend_kernel, plan),
        grid=(rows_n, IMGS_ROW),
        in_specs=[
            pl.BlockSpec((1, ROW, D), lambda r, i: (r, 0, 0)),
            pl.BlockSpec((1, BLOCK, D), lambda r, i: (r, i, 0)),
            whole(gain),
        ]
        + [pl.BlockSpec(memory_space=pltpu.HBM)] * len(pieces),
        out_specs=[near] * 3
        + [
            pl.BlockSpec((1, BLOCK, 2 * D), lambda r, i: (r * IMGS_ROW + i, 0, 0)),
            flat,
            flat,
            pl.BlockSpec(memory_space=pltpu.HBM),
        ],
        out_shape=[
            pltpu.VMEM((images, 16, D), BF16),
            pltpu.VMEM((images, HEADS_PAD, BLOCK), F32),
            pltpu.VMEM((images, 8, D), F32),
            pltpu.HBM((images, BLOCK, 2 * D), BF16),
            pltpu.HBM((rows_n * ROW, D), F32),
            pltpu.HBM((rows_n * ROW, D), BF16),
            pltpu.HBM((D, 4 * D), BF16),
        ],
        scratch_shapes=[
            pltpu.VMEM((BLOCK, 3 * D), BF16),
            pltpu.VMEM((16 * IMGS_ROW, 3 * D), BF16),
            pltpu.VMEM((16 * IMGS_ROW, D), F32),
            pltpu.VMEM((D, 4 * D), BF16),
            pltpu.SemaphoreType.DMA((copies_n,)),
        ],
        compiler_params=params(24),
        cost_estimate=cost(8 * rows_n, 15 * rows_n),
        name="attend",
    )(far(normed), far(resid), gain, *pieces)


def loss_kernel(ids_ref, grads_ref, heads_ref, d_final_ref):
    images = ids_ref.shape[0]
    spread = (
        lax.broadcasted_iota(jnp.int32, (128, CLASSES * TASKS), 1) // TASKS
        == lax.broadcasted_iota(jnp.int32, (128, CLASSES * TASKS), 0)
    ).astype(F32).astype(BF16)
    task_at = lax.broadcasted_iota(jnp.int32, (images, CLASSES * TASKS), 1) % TASKS
    chosen = jnp.where(ids_ref[...] == task_at, dot(grads_ref[...], spread), 0.0).astype(BF16)
    d_final_ref[...] = dot(chosen, heads_ref[...])


def loss_grads(ids, grads, heads):
    operands = (ids, grads, heads)
    out = jax.ShapeDtypeStruct((ids.shape[0], D), F32)
    return pl.pallas_call(
        loss_kernel,
        grid=(1,),
        in_specs=[whole(o) for o in operands],
        out_specs=whole(out),
        out_shape=out,
        compiler_params=params(12),
        cost_estimate=cost(0.1, 2),
        name="loss_grads",
    )(*operands)


def class_kernel(
    plans, d_final_ref, grads_ref, mlp_gain_ref, final_gain_ref,
    queries_ref, probs_ref, middles_ref, kv_hbm, front_hbm, *refs,
):
    feed_refs = refs[:-14]
    (
        sent_ref, weights_ref, routes_ref, d_class_ref, d_middle_ref, up_ref, down_ref,
        score_slots, prob_slots, kv_ref, front_ref, sems, up_sems, down_sems,
    ) = refs[-14:]
    images = middles_ref.shape[0]
    up_copies = make_copies(plans[0](feed_refs, up_ref), up_sems)
    down_copies = make_copies(plans[1](feed_refs, down_ref), down_sems)
    for pair in zip(up_copies, down_copies):
        for copy in pair:
            copy.start()
    front_copy, kv_copy = start_copies([(front_hbm, front_ref), (kv_hbm, kv_ref)], sems)
    mlp_gain, final_gain = mlp_gain_ref[...], final_gain_ref[...]
    middle = middles_ref[:, 0, :]
    unit_mlp, inv_mlp = unit_norm(middle)
    normed = (unit_mlp * mlp_gain).astype(BF16)
    output, pre = middle, []
    width = FF // len(up_copies)
    for at, (up_copy, down_copy) in enumerate(zip(up_copies, down_copies)):
        cols = slice(at * width, (at + 1) * width)
        up_copy.wait()
        pre.append(dot(normed, up_ref[:, cols]))
        down_copy.wait()
        output = output + dot(gelu(pre[-1]).astype(BF16), down_ref[cols, :])
    pre = jnp.concatenate(pre, axis=1)
    unit_fin, inv_fin = unit_norm(output)
    sent_ref[:, 2 * D : 3 * D] = (unit_fin * final_gain).astype(BF16)
    d_output = norm_back(d_final_ref[...], unit_fin, inv_fin, final_gain)
    d_act = dot_t(d_output.astype(BF16), down_ref[...])
    d_pre = (d_act * gelu_slope(pre)).astype(BF16)
    d_middle = d_output + norm_back(dot_t(d_pre, up_ref[...]), unit_mlp, inv_mlp, mlp_gain)
    d_middle_ref[:images] = d_middle
    front_copy.wait()
    d_context = dot_t(d_middle.astype(BF16), front_ref[:, 3 * D :]).astype(BF16)
    sent_ref[:, 3 * D : 4 * D] = d_context
    of_head = head_rows_mask()
    scale = HDIM ** (-0.5)
    kv_copy.wait()
    queries = jnp.concatenate([queries_ref[img, 0:1, :] for img in range(images)], axis=0)
    sent_ref[:, :D] = queries
    spread_heads = lambda rows: (rows[:, None, :] * of_head[None]).reshape(images * HEADS_PAD, D).astype(BF16)
    by_head = spread_heads(d_context.astype(F32))
    probs = probs_ref[...].reshape(images * HEADS_PAD, BLOCK)
    rows_of = lambda array, img: array[img * HEADS_PAD : (img + 1) * HEADS_PAD]
    d_probs = jnp.concatenate(
        [dot_t(rows_of(by_head, img), kv_ref[img, :, D:]) for img in range(images)], axis=0
    )
    d_scores = probs * (d_probs - jnp.sum(probs * d_probs, axis=-1, keepdims=True))
    score_slots[...] = d_scores[:, :128]
    prob_slots[...] = probs[:, :128]
    d_scores = d_scores.astype(BF16)
    weights_ref[:, :HEADS_PAD] = d_scores.reshape(images, HEADS_PAD, BLOCK)
    weights_ref[:, HEADS_PAD:] = probs.astype(BF16).reshape(images, HEADS_PAD, BLOCK)
    d_queries = jnp.concatenate(
        [
            jnp.sum(dot(rows_of(d_scores, img), kv_ref[img, :, :D]) * of_head, axis=0, keepdims=True)
            for img in range(images)
        ],
        axis=0,
    )
    lane = lax.broadcasted_iota(jnp.int32, (images, 128), 1)
    for slots, start in ((prob_slots, D), (score_slots, 4 * D)):
        for pair in range(HEADS // 2):
            first, second = (slots[pl.ds(2 * pair + h, images, stride=HEADS_PAD)] for h in range(2))
            both = jnp.where(lane < SLOTS, first, pltpu.roll(second, SLOTS, 1))
            sent_ref[:, start + pair * 128 : start + (pair + 1) * 128] = both.astype(BF16)
    sent_ref[:, 5 * D :] = grads_ref[...]
    by_key = dot_t(spread_heads(queries.astype(F32) * scale), front_ref[:, D : 2 * D]).astype(BF16)
    by_value = dot_t(by_head, front_ref[:, 2 * D : 3 * D]).astype(BF16)
    routes_ref[:, :HEADS_PAD] = by_key.reshape(images, HEADS_PAD, D)
    routes_ref[:, HEADS_PAD:] = by_value.reshape(images, HEADS_PAD, D)
    d_class_ref[:images] = dot_t((d_queries * scale).astype(BF16), front_ref[:, :D])


SENT = 5 * D + 128


def class_path(d_final, grads, gains, attended, feed_weights):
    images = d_final.shape[0]
    *small, kv, front = attended
    operands = (d_final, grads, *gains[1:], *small)
    feed_arrays, plans, copies_n = feed_weights
    remote = (far(kv), far(front), *feed_arrays)
    outs = [
        jax.ShapeDtypeStruct((images, SENT), BF16),
        jax.ShapeDtypeStruct((images, 2 * HEADS_PAD, BLOCK), BF16),
        jax.ShapeDtypeStruct((images, 2 * HEADS_PAD, D), BF16),
        jax.ShapeDtypeStruct((images + SPARE, D), F32),
        jax.ShapeDtypeStruct((images + SPARE, D), F32),
        pltpu.VMEM((D, FF), BF16),
        pltpu.VMEM((FF, D), BF16),
    ]
    near = pl.BlockSpec(memory_space=pltpu.VMEM)
    return pl.pallas_call(
        functools.partial(class_kernel, plans),
        in_specs=[near] * len(operands) + [pl.BlockSpec(memory_space=pltpu.HBM)] * len(remote),
        out_specs=[near] * len(outs),
        out_shape=outs,
        scratch_shapes=[
            pltpu.VMEM((images * HEADS_PAD, 128), F32),
            pltpu.VMEM((images * HEADS_PAD, 128), F32),
            pltpu.VMEM(kv.shape, BF16),
            pltpu.VMEM((D, 4 * D), BF16),
            pltpu.SemaphoreType.DMA((2,)),
            pltpu.SemaphoreType.DMA((copies_n,)),
            pltpu.SemaphoreType.DMA((copies_n,)),
        ],
        compiler_params=params(24),
        cost_estimate=cost(8, 30),
        name="class_path",
    )(*operands, *remote)


FF_STEP = 768


FEED_IMAGES = 2


def feed_kernel(normed_ref, middle_ref, up_ref, down_ref, *refs):
    out_ref, row_buf = refs[-2:]
    img = pl.program_id(0)
    rows = normed_ref[...]
    total = middle_ref[...]
    for step in range(FF // FF_STEP):
        at = slice(step * FF_STEP, (step + 1) * FF_STEP)
        total = total + dot(gelu(dot(rows, up_ref[:, at])).astype(BF16), down_ref[at, :])
    for at in range(IMGS_ROW // FEED_IMAGES):

        @pl.when(img == at)
        def _():
            for within in range(FEED_IMAGES):
                here = at * FEED_IMAGES + within
                start = within * BLOCK
                row_buf[here * IMG : (here + 1) * IMG] = total[start : start + IMG]
                row_buf[TAIL_AT + here * TAIL : TAIL_AT + (here + 1) * TAIL] = total[start + IMG : start + BLOCK]

    @pl.when(img == IMGS_ROW // FEED_IMAGES - 1)
    def _():
        out_ref[0] = row_buf[:ROW].astype(BF16)


def feed(normed, middle, up_all, down_all, row, rows_n, chain):
    steps = IMGS_ROW // FEED_IMAGES
    spec = pl.BlockSpec((FEED_IMAGES * BLOCK, D), lambda i: (row * steps + i, 0))
    chained = [] if chain is None else [chain]
    return pl.pallas_call(
        feed_kernel,
        grid=(steps,),
        in_specs=[spec, spec]
        + [pl.BlockSpec(memory_space=pltpu.VMEM)] * 2
        + [pl.BlockSpec(memory_space=pltpu.HBM)] * len(chained),
        out_specs=pl.BlockSpec((1, ROW, D), lambda i: (row, 0, 0)),
        out_shape=pltpu.HBM((rows_n, ROW, D), BF16),
        input_output_aliases={} if chain is None else {4: 0},
        scratch_shapes=[pltpu.VMEM((ROW + SPARE, D), F32)],
        compiler_params=params(28),
        cost_estimate=cost(10, 20),
        name="feed",
    )(far(normed), far(middle), up_all, down_all, *chained)


def token_grads_kernel(resid_ref, weights_ref, routes_ref, d_class_ref, d_middle_ref, gain_ref, out_ref):
    row_at = pl.program_id(0)
    gain = gain_ref[...]
    place = lax.broadcasted_iota(jnp.int32, (BLOCK, 1), 0)
    is_class = (place == 0).astype(F32)
    keep = jnp.where((place == 0) | (place > PROMPTS), 1.0, 0.0)
    zeros_at = TAIL_AT // 8 * 8
    out_ref[0, zeros_at:] = jnp.zeros((ROW - zeros_at, D), F32)
    for img in range(IMGS_ROW):
        one = pl.ds(row_at * IMGS_ROW + img, 1)
        unit_rows, inv_std = unit_norm(resid_ref[0, img * BLOCK : (img + 1) * BLOCK].astype(F32))
        d_normed = lax.dot_general(
            weights_ref[img], routes_ref[img], (((0,), (0,)), ((), ())), preferred_element_type=F32
        )
        d_normed = d_normed + is_class * d_class_ref[one]
        d_resid = norm_back(d_normed, unit_rows, inv_std, gain) + is_class * d_middle_ref[one]
        out_ref[0, img * IMG : (img + 1) * IMG] = (d_resid * keep)[:IMG]


def token_grads(resid, weights, routes, d_class, d_middle, gain):
    rows_n = resid.shape[0]
    row_spec = pl.BlockSpec((1, ROW, D), lambda r: (r, 0, 0))
    img_spec = lambda width: pl.BlockSpec((IMGS_ROW, 2 * HEADS_PAD, width), lambda r: (r, 0, 0))
    return pl.pallas_call(
        token_grads_kernel,
        grid=(rows_n,),
        in_specs=[row_spec, img_spec(BLOCK), img_spec(D), whole(d_class), whole(d_middle), whole(gain)],
        out_specs=row_spec,
        out_shape=pltpu.HBM(resid.shape, F32),
        compiler_params=params(20),
        cost_estimate=cost(0.5, 20),
        name="token_grads",
    )(far(resid), weights, routes, d_class, d_middle, gain)


def sums_kernel(front_ref, prompts_ref, gain_ref, *refs):
    parts, (prompt_out, head_out, all_buf, sum_buf, prompt_buf, sems) = refs[:-6], refs[-6:]
    rows = parts[0].shape[0]
    run_copies([(part, all_buf.at[pl.ds(at * rows, rows), :]) for at, part in enumerate(parts)], sems)
    scale = np.float32(HDIM ** (-0.5)).astype(BF16)
    column = lambda at: all_buf[:, at * D : (at + 1) * D]
    by_class = all_buf[:, 5 * D :].T
    ids = by_class[CLASSES : CLASSES + 1].astype(F32)
    masks = [(ids == task).astype(F32).astype(BF16) for task in range(TASKS)]
    of_task = (lax.broadcasted_iota(jnp.int32, (TASKS, 1), 0).astype(F32) == ids).astype(F32)
    spread = by_class[:CLASSES].astype(F32)[:, None, :] * of_task[None]
    head_out[...] = dot(spread.reshape(CLASSES * TASKS, -1).astype(BF16), column(2))
    lane = lax.broadcasted_iota(jnp.int32, (SLOTS, 128), 1)
    for side, (slots, lane_rows) in enumerate(((column(4), column(0) * scale), (column(1), column(3)))):
        slots = slots.T
        for pair in range(HEADS // 2):
            at = slice(pair * 128, (pair + 1) * 128)
            summed = dot(jnp.concatenate([slots[at] * mask for mask in masks], axis=0), lane_rows[:, at])
            for task in range(TASKS):
                first, second = (summed[task * 128 + h * SLOTS : task * 128 + (h + 1) * SLOTS] for h in range(2))
                sum_buf[task * SLOTS : (task + 1) * SLOTS, side * D + pair * 128 : side * D + (pair + 1) * 128] = (
                    jnp.where(lane < HDIM, first, second).astype(BF16)
                )
    d_normed = dot_t(sum_buf[...], front_ref[:, D : 3 * D])
    by_lanes(prompt_buf, prompts_ref[...].astype(F32))
    for task in range(TASKS):
        unit_rows, inv_std = unit_norm(read_strided(prompt_buf, task, PROMPTS))
        d_task = d_normed[task * SLOTS + 1 : task * SLOTS + 1 + PROMPTS]
        write_strided(prompt_buf, task, norm_back(d_task, unit_rows, inv_std, gain_ref[...]))
    for block, lanes in enumerate(LANE_BLOCKS):
        prompt_out[:, lanes] = prompt_buf[block, : PROMPTS * TASKS]


def sums(front, prompts, gain, parts):
    operands = (front, prompts, gain)
    outs = [
        jax.ShapeDtypeStruct((PROMPTS * TASKS, D), F32),
        jax.ShapeDtypeStruct((CLASSES * TASKS, D), F32),
    ]
    images = sum(part.shape[0] for part in parts)
    return pl.pallas_call(
        sums_kernel,
        grid=(1,),
        in_specs=[pl.BlockSpec(memory_space=pltpu.VMEM)] * len(operands)
        + [pl.BlockSpec(memory_space=pl.ANY)] * len(parts),
        out_specs=[whole(o) for o in outs],
        out_shape=outs,
        scratch_shapes=[
            pltpu.VMEM((images, SENT), BF16),
            pltpu.VMEM((TASKS * SLOTS, 2 * D), BF16),
            pltpu.VMEM((len(LANE_BLOCKS), STRIDED_ROWS, LANES), F32),
            pltpu.SemaphoreType.DMA((len(parts),)),
        ],
        compiler_params=params(28 if images <= 512 else 60),
        cost_estimate=cost(5, 15),
        name="sums",
    )(*operands, *parts)


def gather_rows(shard, dp):
    part = shard.shape[0] // dp
    mine = lax.dynamic_slice_in_dim(shard, lax.axis_index("dp") * part, part, 0)
    return lax.all_gather(mine, ("fsdp", "dp"), axis=0, tiled=True)


def copy_whole(at):
    return lambda refs, dst: [(refs[at], dst)]


def places():
    d, f = lax.axis_index("dp"), lax.axis_index("fsdp")
    return d // 2, d % 2, f // 2, f % 2


def exchange(value, dy=0, dc=0, dz=0, dx=0):
    pairs = []
    for at in range(32):
        y, c, z, x = at // 16, at // 8 % 2, at // 2 % 4, at % 2
        pairs.append((at, (((y ^ dy) * 2 + (c ^ dc)) * 4 + (z ^ dz)) * 2 + (x ^ dx)))
    return lax.ppermute(value, ("dp", "fsdp"), pairs)


HALF_COLS = 2 * D


class Fetch:
    def __init__(self, own, mine, both, cut):
        self.own, self.mine, self.both, self.cut, self.half = own, mine, both, cut, mine.shape[0]

    def along_z(self):
        self.column = jnp.concatenate([exchange(self.mine, dz=r) for r in (1, 2, 3)], axis=0)

    def beside(self):
        self.own_x = exchange(self.both, dx=1)

    def across(self):
        self.over_x = exchange(self.column, dx=1)
        self.over_y = exchange(self.column, dy=1)

    def diagonal(self):
        self.diag_y = exchange(self.over_x[: self.cut], dy=1)
        self.diag_x = exchange(self.over_y[self.cut :], dx=1)

    def pieces(self):
        near = [self.own_x, self.column, self.over_x, self.over_y, self.diag_y, self.diag_x]
        return self.own + near + [exchange(piece, dc=1) for piece in near]

    def plan(self, refs, dst, put):
        y, c, z, x = places()
        half, cut = self.half, self.cut
        pairs = []
        for side in range(2):
            own_x, column, over_x, over_y, diag_y, diag_x = refs[6 * side : 6 + 6 * side]

            def add(ref, start, count, r, x_at, y_at, within=0):
                return put(ref, start, count, dst, (z ^ r) * 2 + x_at, y_at, c ^ side, within)

            for y_at in range(2):
                pairs += add(own_x, y_at * half, half, 0, x ^ 1, y_at)
            for r in (1, 2, 3):
                start = (r - 1) * half
                pairs += add(column, start, half, r, x, y)
                pairs += add(over_x, start, half, r, x ^ 1, y)
                pairs += add(over_y, start, half, r, x, y ^ 1)
                first = min(max(cut - start, 0), half)
                if first:
                    pairs += add(diag_y, start, first, r, x ^ 1, y ^ 1)
                if first < half:
                    pairs += add(diag_x, start + first - cut, half - first, r, x ^ 1, y ^ 1, first)
        return pairs


def own_rows(ref, dst):
    _, _, z, x = places()
    count = ref.shape[0]
    return [(ref, dst.at[pl.ds(pl.multiple_of((z * 2 + x) * count, count), count), :])]


def put_front(ref, start, count, dst, place, y, c, within):
    row = pl.multiple_of(place * 96 + y * 48 + within, 16)
    cols = pl.ds(pl.multiple_of(c * HALF_COLS, 128), HALF_COLS)
    return [(ref.at[pl.ds(start, count), :], dst.at[pl.ds(row, count), cols])]


def front_bundle(shard):
    y, c, _, _ = places()
    mine = lax.dynamic_slice(shard, (y * 48, c * HALF_COLS), (48, HALF_COLS))
    both = lax.dynamic_slice(shard, (0, c * HALF_COLS), (96, HALF_COLS))
    return Fetch([shard], mine, both, 80)


def fetch_rest(up_shard, down_shard):
    d = lax.axis_index("dp")
    up_part = lax.dynamic_slice(up_shard, (0, d * D), (96, D))
    down_part = lax.dynamic_slice_in_dim(down_shard, d * 96, 96, 0)
    gathered = lax.all_gather(jnp.concatenate([up_part, down_part], axis=0), ("fsdp", "dp"), axis=0)
    gathered = gathered.reshape(8, 4, 192, D)

    def up_plan(refs, dst):
        dst = dst.reshape(8, 96, FF)
        return [(refs[0].at[:, d, 0:96, :], dst.at[:, :, D * d : D * d + D]) for d in range(4)]

    def down_plan(refs, dst):
        dst = dst.reshape(8, 4, 96, D)
        return [(refs[0].at[2 * d : 2 * d + 2, :, 96:192, :], dst.at[2 * d : 2 * d + 2]) for d in range(4)]

    return [far(gathered)], (up_plan, down_plan), 4


def share_rows(rows, works):
    parts, done = [rows], None
    for work, shifts in zip(works, ([dict(dz=r) for r in (1, 2, 3)], [dict(dx=1)], [dict(dy=1), dict(dc=1)])):
        rows = jnp.concatenate(parts, axis=0) if len(parts) > 1 else rows
        if done is not None:
            rows, done = lax.optimization_barrier((rows, done))
        parts = [rows] + [exchange(rows, **shift) for shift in shifts]
        done = work(done)
    near, across, core = parts
    across, done = lax.optimization_barrier((across, done))
    return [near, across, core, exchange(across, dc=1)], done


def body(
    tuned, dp, tokens, task_ids, logit_grads, prompts, head_weights, qkv_weight, out_weight, up_weight, down_weight,
    attn_gain, mlp_gain, final_gain,
):
    rows_n = tokens.shape[0] * tokens.shape[1]
    images = rows_n * IMGS_ROW
    front_shard = jnp.concatenate([qkv_weight, out_weight], axis=1)
    gains = [gain.reshape(1, D) for gain in (attn_gain, mlp_gain, final_gain)]
    ids = task_ids.reshape(rows_n, IMGS_ROW)
    prompt_rows = prompts.transpose(1, 0, 2).reshape(PROMPTS * TASKS, D)
    token_rows = tokens.reshape(rows_n, ROW, D)
    ids_col = ids.reshape(images, 1)
    head_rows = head_weights.transpose(2, 0, 1).reshape(CLASSES * TASKS, D)
    grads = jnp.concatenate(
        [logit_grads.reshape(images, CLASSES), jnp.broadcast_to(ids_col, (images, 128 - CLASSES)).astype(BF16)], axis=1
    )
    tie = lambda *values: lax.optimization_barrier(values)
    if tuned:
        feed_weights = fetch_rest(up_weight, down_weight)
        front_in = front_bundle(front_shard)
        front_in.along_z()
        front_in.beside()
        resid, normed = assemble(ids, token_rows, prompt_rows, gains[0])
        front_in.column, normed = tie(front_in.column, normed)
        front_in.across()
        front_in.diagonal()
        plan_front = lambda refs, dst: own_rows(refs[0], dst) + front_in.plan(refs[1:], dst, put_front)
        fetched = [far(piece) for piece in front_in.pieces()], plan_front, 1 + 2 * (2 + 9 + 4)
    else:
        feed_weights = [gather_rows(w, dp) for w in (up_weight, down_weight)], (copy_whole(0), copy_whole(1)), 1
        resid, normed = assemble(ids, token_rows, prompt_rows, gains[0])
        fetched = [gather_rows(front_shard, dp)], copy_whole(0), 1
    *attended, middle, normed_two, front = attend(normed, resid, gains[1], *fetched)
    sent, weights, routes, d_class, d_middle, up_all, down_all = class_path(
        loss_grads(ids_col, grads, head_rows), grads, gains, [*attended, front], feed_weights
    )

    def feed_rows(rows, chain):
        for row in rows:
            chain = feed(normed_two, middle, up_all, down_all, row, rows_n, chain)
        return chain

    works = (
        lambda done: (token_grads(resid, weights, routes, d_class, d_middle, gains[0]), None),
        lambda done: (done[0], feed_rows(range(rows_n // 2), None)),
        lambda done: (done[0], feed_rows(range(rows_n // 2, rows_n), done[1])),
    )
    if tuned:
        parts, (input_grads, activations) = share_rows(sent, works)
    else:
        parts = [lax.all_gather(sent, ("dp", "fsdp"), axis=0, tiled=True)]
        input_grads, activations = works[2](works[1](works[0](None)))
    prompt_out, head_out = sums(front, prompt_rows, gains[0], parts)
    return (
        activations.reshape(tokens.shape),
        input_grads.reshape(tokens.shape),
        prompt_out.reshape(PROMPTS, TASKS, D).transpose(1, 0, 2),
        head_out.reshape(CLASSES, TASKS, D).transpose(1, 2, 0),
    )


def solution(mesh):
    rows = P(None, ("dp", "fsdp"), None, None)
    in_specs = (rows, P(None, ("dp", "fsdp"), None), rows, P(), P(), *(P("fsdp", None),) * 4, P(), P(), P())
    return jax.shard_map(
        functools.partial(body, dict(mesh.shape) == {"dp": 4, "fsdp": 8}, mesh.shape["dp"]),
        mesh=mesh,
        in_specs=in_specs,
        out_specs=(rows, rows, P(), P()),
        check_vma=False,
    )
```
